256 devices in a mesh: dp: 16 (over x, y), tensor: 8 (over z), side: 2 (over core).
Axes of the slice: x: 4, y: 4, z: 8, core: 2. Of those that a mesh axis runs over, the one named last changes fastest.
Arguments:
- q_new: bfloat16 [1024, 6144], P(('dp', 'side'), 'tensor'), may hold values from -6 to 6
- k_new: bfloat16 [1024, 1024], P(('dp', 'side'), 'tensor'), may hold values from -6 to 6
- v_new: bfloat16 [1024, 1024], P(('dp', 'side'), 'tensor'), may hold values from -6 to 6
- k_cache: bfloat16 [1024, 192, 1024], P(('dp', 'side'), None, 'tensor'), may hold values from -6 to 6
- v_cache: bfloat16 [1024, 192, 1024], P(('dp', 'side'), None, 'tensor'), may hold values from -6 to 6
- lengths: int32 [1024], P(('dp', 'side')), may hold values from 24 to 192, as said below
- attn_out_weight: bfloat16 [6144, 6144], P('tensor', ('dp', 'side')), may hold values from -0.078125 to 0.078125
- residual: bfloat16 [1024, 6144], P('tensor', ('dp', 'side')), may hold values from -1.5 to 1.5
- norm_gain: float32 [6144], replicated, may hold values from 0.1 to 1.9
- router_weight: bfloat16 [6144, 8], replicated, may hold values from -0.02734375 to 0.02734375
- expert_ids: int32 [1024, 2], replicated, may hold values from 0 to 7, all different within a row; in each aligned block of 128 rows (0 to 127, 128 to 255, ...) at most 64 rows name the same one
- gate_weight: bfloat16 [8, 6144, 8192], P('tensor', None, ('dp', 'side')), may hold values from -0.078125 to 0.078125
- up_weight: bfloat16 [8, 6144, 8192], P('tensor', None, ('dp', 'side')), may hold values from -0.078125 to 0.078125
- down_weight: bfloat16 [8, 8192, 6144], P('tensor', ('dp', 'side')), may hold values from -0.0625 to 0.0625
Outputs:
- layer_out: bfloat16 [1024, 6144], P('tensor', ('dp', 'side'))
The draws below stay inside these ranges and needn't reach their ends.
Inputs may be any that keep to these rules, and one draw needn't show every extreme that they name: `expert_ids`: each row names two different experts; in each aligned block of 128 rows no expert is named by more than 64 rows, and in every draw some expert is named by exactly 64 rows of a block. Row r attends to cached positions 0 to lengths[r] - 1 and to its new key; some rows hold all 192.
All inputs are finite; a program needn't handle non-finite values.
Results may differ from the reference program's by a relative error of at most 0.035.
Values may be sent and summed in bfloat16 or wider, within the bound.
No kernel may reach another device: no remote copies, remote signals or barrier semaphores. Data moves between devices by JAX's collectives and lax.ppermute only.
A program may use at most 128 MiB of HBM per device.

```python
import math
import jax
import jax.numpy as jnp
import numpy as np
from jax import lax

D = 6144
HEADS = 48
KV_HEADS = 8
HEAD_DIM = 128
EXPERTS = 8
TOP = 2
HID = 8192
CTX = 192
ROWS = 1024
RB = 128
MOST = 64
N_TENSOR = 8


def draw_q_new(key, part):
    drawn = jnp.clip(jax.random.normal(jax.random.fold_in(key, 1), (ROWS, HEADS * HEAD_DIM), jnp.float32), -6.0, 6.0)
    return drawn.astype(jnp.bfloat16)


def draw_k_cache(key, part):
    drawn = jnp.clip(jax.random.normal(jax.random.fold_in(key, 2), (ROWS, CTX, KV_HEADS * HEAD_DIM), jnp.float32), -6.0, 6.0)
    return drawn.astype(jnp.bfloat16)


def draw_lengths(key, part):
    drawn = jax.random.randint(jax.random.fold_in(key, 3), (ROWS,), CTX // 8, CTX + 1, dtype=jnp.int32)
    row_index = jnp.arange(ROWS, dtype=jnp.int32)
    return jnp.where(row_index % 16 == 5, CTX, drawn).astype(jnp.int32)


def level_of(rng, dims, cuts, low, top_value):
    loudness, own = 1.0, jax.random.fold_in(rng, 6)
    for dim, blocks in cuts:
        draws = jnp.exp(jax.random.uniform(jax.random.fold_in(own, dim), (blocks,), jnp.float32, low / len(cuts), top_value / len(cuts)))
        loudness = loudness * jnp.repeat(draws, dims[dim] // blocks).reshape([-1 if axis == dim else 1 for axis in range(len(dims))])
    return loudness


def deal_out(rng, own, number, rows, count, top, bound, lean):
    ranking = jax.random.permutation(rng, count)
    packed, ordinary = load_shares(count, rows * top, bound, lean, True), load_shares(count, rows * top, bound, lean, False)
    places = jnp.arange(count)

    def named(tallies, offset_by):
        used = int((tallies > 0).sum())
        fixed = max(1, used // 4)
        passed = fixed + (places - fixed + offset_by * (used - fixed)) % max(1, count - fixed)
        return jnp.zeros((count,), jnp.int32).at[ranking[jnp.where(places < fixed, places, passed)]].set(jnp.asarray(tallies, jnp.int32))

    tallies = jnp.where(number % 4 == 0, named(packed, number // 4), named(ordinary, number - number // 4 - 1))
    mixed = jax.random.permutation(jax.random.fold_in(own, 3), count)
    donor, taker = mixed[0:count // 2 * 2:2], mixed[1:count // 2 * 2:2]
    room = jnp.minimum(tallies[donor] - 1, bound - tallies[taker]) // 2
    room = jnp.where((donor == ranking[0]) | (taker == ranking[0]) | (tallies[taker] == 0), 0, jnp.maximum(room, 0))
    passed = jax.random.randint(jax.random.fold_in(own, 4), (count // 2,), 0, 1 << 20) % (room + 1)
    tallies = tallies.at[donor].add(-passed).at[taker].add(passed)
    items = jnp.searchsorted(jnp.cumsum(tallies), jnp.arange(rows * top), side="right").astype(jnp.int32)
    listing = items.reshape(top, rows).T
    listing = listing[jax.random.permutation(jax.random.fold_in(own, 1), rows)]
    offset_by = jax.random.randint(jax.random.fold_in(own, 2), (rows, 1), 0, top)
    return jnp.take_along_axis(listing, (jnp.arange(top)[None, :] + offset_by) % top, axis=1)


def load_shares(number_of, total, most, slope, full):
    portions = [(1 << 20) // math.isqrt(grade ** slope) + 1 for grade in range(1, number_of + 1)]
    largest = most if full else min(most, max(-(-total // number_of), total * portions[0] // sum(portions)))
    least = 1 if total - largest >= number_of - 1 else 0
    holding, rest = [largest] + [least] * (number_of - 1), total - largest - least * (number_of - 1)
    while rest > 0:
        movable = [i for i in range(1, number_of) if holding[i] < largest] or [i for i in range(1, number_of) if holding[i] < most]
        whole, left = sum([portions[i] for i in movable]), rest
        for i in movable:
            extra = min(most - holding[i], max(1, left * portions[i] // whole), rest)
            holding[i] = holding[i] + extra
            rest = rest - extra
    return np.array(holding)


def noise(rng, shape, scale, limit, cuts=(), kind=jnp.bfloat16):
    values = jax.random.normal(rng, shape, jnp.float32) * scale
    if len(cuts) > 0:
        values = level_of(rng, shape, cuts, -0.22, 0.18) * values
    return jnp.clip(values, min=-limit, max=limit).astype(kind)


def setup_inputs(seed: int = 0) -> dict:
    arg_keys = jax.random.split(jax.random.key(seed), 15)
    q_new = draw_q_new(jax.random.fold_in(arg_keys[14], 71), 0)
    k_new = noise(arg_keys[1], (ROWS, KV_HEADS * HEAD_DIM), 1.0, 6.0, ((0, 32), (1, 8)))
    v_new = noise(arg_keys[2], (ROWS, KV_HEADS * HEAD_DIM), 1.0, 6.0, ((0, 32), (1, 8)))
    k_cache = draw_k_cache(jax.random.fold_in(arg_keys[14], 71), 0)
    v_cache = noise(arg_keys[4], (ROWS, CTX, KV_HEADS * HEAD_DIM), 1.0, 6.0, ((0, 32), (2, 8)))
    lengths = draw_lengths(jax.random.fold_in(arg_keys[14], 71), 0)
    attn_out_weight = noise(arg_keys[6], (HEADS * HEAD_DIM, D), (HEADS * HEAD_DIM) ** -0.5, 0.078125, ((0, 8), (1, 32)))
    residual = noise(arg_keys[7], (ROWS, D), 0.1, 1.5, ((0, 8), (1, 32)))
    norm_gain = jnp.clip(1.0 + 0.18 * jax.random.normal(arg_keys[8], (D,), jnp.float32), 0.1, 1.9)
    router_weight = noise(arg_keys[9], (D, EXPERTS), (D * 9) ** -0.5, 0.02734375)
    expert_ids_keys = jax.random.split(jax.random.fold_in(arg_keys[10], 1), ROWS // RB)
    expert_ids_turns = jax.random.permutation(jax.random.fold_in(arg_keys[10], 3), ROWS // RB)
    expert_ids = jax.vmap(lambda own, number: deal_out(jax.random.fold_in(arg_keys[10], 2), own, number, RB, EXPERTS, TOP, MOST, 3))(expert_ids_keys, expert_ids_turns).reshape((ROWS, TOP))
    gate_weight = noise(arg_keys[11], (EXPERTS, D, HID), D ** -0.5, 0.078125, ((0, 8), (2, 32)))
    up_weight = noise(arg_keys[12], (EXPERTS, D, HID), D ** -0.5, 0.078125, ((0, 8), (2, 32)))
    down_weight = noise(arg_keys[13], (EXPERTS, HID, D), HID ** -0.5, 0.0625, ((0, 8), (1, 32)))
    return dict(q_new=q_new, k_new=k_new, v_new=v_new, k_cache=k_cache, v_cache=v_cache, lengths=lengths, attn_out_weight=attn_out_weight, residual=residual, norm_gain=norm_gain, router_weight=router_weight, expert_ids=expert_ids, gate_weight=gate_weight, up_weight=up_weight, down_weight=down_weight)


eps = 1e-05

def slot_tables(expert_ids, experts, blocks, most):
    rows = expert_ids.shape[0]
    block_rows = rows // blocks
    labels = jnp.arange(experts, dtype=jnp.int32)
    chosen = (expert_ids[:, :, None] == labels[None, None, :]).astype(jnp.int32)
    member = lax.optimization_barrier(jnp.sum(chosen, axis=1)).astype(jnp.int32)
    ranks = jnp.cumsum(member.reshape(blocks, block_rows, experts), axis=1).astype(jnp.int32)
    ranks = ranks.reshape(rows, experts) - 1
    block_of = jnp.arange(rows, dtype=jnp.int32) // block_rows
    slots = block_of[:, None] * most + ranks
    picked = lax.optimization_barrier(jnp.sum(chosen * slots[:, None, :], axis=2)).astype(jnp.int32)
    capacity = blocks * most
    row_ids = jnp.broadcast_to(jnp.arange(rows, dtype=jnp.int32)[:, None], (rows, 2))
    others = expert_ids[:, ::-1]
    leads = jnp.broadcast_to(jnp.array([1, 0], dtype=jnp.int32)[None, :], (rows, 2))
    table = jnp.full((experts, capacity), rows, jnp.int32).at[expert_ids, picked].set(row_ids)
    partner = jnp.zeros((experts, capacity), jnp.int32).at[expert_ids, picked].set(others)
    leading = jnp.zeros((experts, capacity), jnp.int32).at[expert_ids, picked].set(leads)
    return (picked, table, partner, leading)

def reference(q_new, k_new, v_new, k_cache, v_cache, lengths, attn_out_weight, residual, norm_gain, router_weight, expert_ids, gate_weight, up_weight, down_weight):
    group_size = HEADS // KV_HEADS
    inv_root = HEAD_DIM ** (-0.5)
    queries = q_new.astype(jnp.float32).reshape(ROWS, KV_HEADS, group_size, HEAD_DIM)
    cache_keys = k_cache.astype(jnp.float32).reshape(ROWS, CTX, KV_HEADS, HEAD_DIM)
    cache_values = v_cache.astype(jnp.float32).reshape(ROWS, CTX, KV_HEADS, HEAD_DIM)
    own_keys = k_new.astype(jnp.float32).reshape(ROWS, KV_HEADS, HEAD_DIM)
    own_values = v_new.astype(jnp.float32).reshape(ROWS, KV_HEADS, HEAD_DIM)
    cache_scores = jnp.einsum('rkgd,rckd->rkgc', queries, cache_keys) * inv_root
    own_scores = jnp.einsum('rkgd,rkd->rkg', queries, own_keys) * inv_root
    live_mask = (jnp.arange(CTX, dtype=jnp.int32)[None, :] < lengths[:, None])[:, None, None, :]
    cache_scores = jnp.where(live_mask, cache_scores, -1e+30)
    peak = jnp.maximum(lax.optimization_barrier(jnp.max(cache_scores, axis=3)), own_scores)
    cache_exp = jnp.exp(cache_scores - peak[..., None])
    own_exp = jnp.exp(own_scores - peak)
    denominator = lax.optimization_barrier(jnp.sum(cache_exp, axis=3)) + own_exp
    cache_weights = lax.optimization_barrier((cache_exp / denominator[..., None]).astype(jnp.bfloat16)).astype(jnp.float32)
    own_weights = lax.optimization_barrier((own_exp / denominator).astype(jnp.bfloat16)).astype(jnp.float32)
    mixed_heads = jnp.einsum('rkgc,rckd->rkgd', cache_weights, cache_values) + own_weights[..., None] * own_values[:, :, None, :]
    attention = mixed_heads.reshape(ROWS, HEADS * HEAD_DIM).astype(jnp.bfloat16)
    hidden = (residual.astype(jnp.float32) + jnp.dot(attention, attn_out_weight, preferred_element_type=jnp.float32)).astype(jnp.bfloat16)
    hidden_f = hidden.astype(jnp.float32)
    normed = (hidden_f * lax.rsqrt(lax.optimization_barrier(jnp.mean(hidden_f * hidden_f, axis=1, keepdims=True)) + eps) * norm_gain).astype(jnp.bfloat16)
    logits = jnp.dot(normed, router_weight, preferred_element_type=jnp.float32)
    first_logit = jnp.take_along_axis(logits, expert_ids[:, 0:1], axis=1)[:, 0]
    second_logit = jnp.take_along_axis(logits, expert_ids[:, 1:2], axis=1)[:, 0]
    shares = jnp.stack([jax.nn.sigmoid(first_logit - second_logit), jax.nn.sigmoid(second_logit - first_logit)], axis=1)
    picked, table, partner, leading = slot_tables(expert_ids, EXPERTS, N_TENSOR, MOST)

    def expert_run(expert):
        rows_in = jnp.take(normed, table[expert], axis=0, mode='fill', fill_value=0)
        gate = jnp.dot(rows_in, gate_weight[expert], preferred_element_type=jnp.float32)
        upward = jnp.dot(rows_in, up_weight[expert], preferred_element_type=jnp.float32)
        inner = (jax.nn.silu(gate) * upward).astype(jnp.bfloat16)
        return jnp.dot(inner, down_weight[expert], preferred_element_type=jnp.float32)
    expert_outs = lax.map(expert_run, jnp.arange(EXPERTS, dtype=jnp.int32))
    chosen_out = expert_outs[expert_ids, picked]
    parts = lax.optimization_barrier((shares[..., None] * chosen_out).astype(jnp.bfloat16)).astype(jnp.float32)
    return (hidden_f + parts[:, 0] + parts[:, 1]).astype(jnp.bfloat16)
```

```python
import jax
import jax.numpy as jnp
from jax import lax
from jax.experimental import pallas as pl
from jax.experimental.pallas import tpu as pltpu
from jax.sharding import PartitionSpec as P

HEAD_DIM = 128
EXPERTS = 8
eps = 1e-05
F32 = jnp.float32
BF16 = jnp.bfloat16
VMEM_LIMIT = 48 * 1024 * 1024

SHIFT_X = [[(4 * x + y, 4 * ((x + d) % 4) + y) for x in range(4) for y in range(4)] for d in range(4)]
SHIFT_Y = [[(4 * x + y, 4 * x + (y + d) % 4) for x in range(4) for y in range(4)] for d in range(4)]
SWAP = [(0, 1), (1, 0)]


def swap_cores(a):
    return lax.ppermute(a, "side", SWAP)


def gather_xy(a, b):
    a_in = [lax.ppermute(a, "dp", SHIFT_X[d]) for d in (1, 2, 3)]
    b_in = [lax.ppermute(b, "dp", SHIFT_Y[d]) for d in (1, 2, 3)]
    ga = jnp.stack([a] + a_in)
    gb = jnp.stack([b] + b_in)
    first = [ga] + [lax.ppermute(ga, "dp", SHIFT_Y[d]) for d in (1, 2, 3)]
    second = [gb] + [lax.ppermute(gb, "dp", SHIFT_X[d]) for d in (1, 2, 3)]
    return first, second


def outproj_kernel(pos, own, other, w, out):
    x, y, c = pos[0], pos[1], pos[2]
    for ref, side in ((own, c), (other, 1 - c)):
        for h in range(2):
            sums = jnp.dot(
                ref[h].reshape(256, 768), w[...], preferred_element_type=F32
            ).astype(BF16)
            for k in range(16):
                dx, dy = (k % 4, k // 4) if h == 0 else (k // 4, k % 4)
                chip = ((x - dx) & 3) * 4 + ((y - dy) & 3)
                row = pl.multiple_of((chip * 2 + side) * 32 + h * 16, 16)
                out[pl.ds(row, 16), :] = sums[k * 16 : k * 16 + 16]


def norm_kernel(pos, a0, a1, a2, a3, b0, b1, b2, b3, gain, out):
    x, y = pos[0], pos[1]
    for h, refs in ((0, (a0, a1, a2, a3)), (1, (b0, b1, b2, b3))):
        for r0 in range(0, 128, 32):
            squares = jnp.zeros((32, 384), F32)
            for i in range(4):
                for j in range(4):
                    v = refs[i][j, r0 : r0 + 32, :].astype(F32)
                    squares = squares + v * v
            mean = jnp.sum(squares, axis=1, keepdims=True) * (1.0 / 6144.0)
            scale = lax.rsqrt(mean + eps)
            for i in range(4):
                for j in range(4):
                    dx, dy = (j, i) if h == 0 else (i, j)
                    chip = ((x - dx) & 3) * 4 + ((y - dy) & 3)
                    v = refs[i][j, r0 : r0 + 32, :].astype(F32)
                    out[chip, h * 128 + r0 : h * 128 + r0 + 32, :] = (
                        v * scale * gain[chip]
                    ).astype(BF16)


def expert_kernel(xn, gate_w, up_w, router, inner, logits, gate, up, logit):
    k = pl.program_id(0)

    @pl.when(k == 0)
    def _():
        gate[...] = jnp.zeros_like(gate)
        up[...] = jnp.zeros_like(up)
        logit[...] = jnp.zeros_like(logit)

    for j in range(4):
        rows = slice(j * 384, j * 384 + 384)
        v = xn[j]
        gate[...] += jnp.dot(v, gate_w[rows, :], preferred_element_type=F32)
        up[...] += jnp.dot(v, up_w[rows, :], preferred_element_type=F32)
        logit[...] += jnp.dot(v, router[rows, :], preferred_element_type=F32)

    @pl.when(k == pl.num_programs(0) - 1)
    def _():
        g = gate[...]
        inner[...] = (g / (1.0 + jnp.exp(-g)) * up[...]).astype(BF16)
        logits[...] = logit[...]


def expert_call(xn, gate_w, up_w, router):
    return pl.pallas_call(
        expert_kernel,
        grid=(4,),
        in_specs=[
            pl.BlockSpec((4, 256, 384), lambda k: (k, 0, 0)),
            pl.BlockSpec((1536, 256), lambda k: (k, 0)),
            pl.BlockSpec((1536, 256), lambda k: (k, 0)),
            pl.BlockSpec((1536, EXPERTS), lambda k: (k, 0)),
        ],
        out_specs=[
            pl.BlockSpec((256, 256), lambda k: (0, 0)),
            pl.BlockSpec((256, EXPERTS), lambda k: (0, 0)),
        ],
        out_shape=[
            jax.ShapeDtypeStruct((256, 256), BF16),
            jax.ShapeDtypeStruct((256, EXPERTS), F32),
        ],
        scratch_shapes=[
            pltpu.VMEM((256, 256), F32),
            pltpu.VMEM((256, 256), F32),
            pltpu.VMEM((256, EXPERTS), F32),
        ],
        compiler_params=pltpu.CompilerParams(vmem_limit_bytes=VMEM_LIMIT),
        name="expert_in",
    )(xn, gate_w, up_w, router)


def down_kernel(pos, inner, w, out_a, out_b):
    sums = jnp.dot(inner[...], w[...], preferred_element_type=F32).astype(BF16)
    out_a[0, 0] = sums[:128]
    out_b[0, 0] = sums[128:]


def down_call(pos, inner, down_w):
    return pl.pallas_call(
        down_kernel,
        grid_spec=pltpu.PrefetchScalarGridSpec(
            num_scalar_prefetch=1,
            grid=(4, 4),
            in_specs=[
                pl.BlockSpec((256, 256), lambda i, j, pos: (0, 0)),
                pl.BlockSpec(
                    (256, 384),
                    lambda i, j, pos: (0, ((pos[0] + j) & 3) * 4 + ((pos[1] + i) & 3)),
                ),
            ],
            out_specs=[
                pl.BlockSpec((1, 1, 128, 384), lambda i, j, pos: (i, j, 0, 0)),
                pl.BlockSpec((1, 1, 128, 384), lambda i, j, pos: (j, i, 0, 0)),
            ],
        ),
        out_shape=[jax.ShapeDtypeStruct((4, 4, 128, 384), BF16)] * 2,
        compiler_params=pltpu.CompilerParams(vmem_limit_bytes=VMEM_LIMIT),
        name="expert_down",
    )(pos, inner, down_w)


def attend(q_new, k_new, v_new, k_cache, v_cache, lengths):
    rows_dev = q_new.shape[0]
    kv_local = k_new.shape[1] // HEAD_DIM
    heads_local = q_new.shape[1] // HEAD_DIM
    group_size = heads_local // kv_local
    cache_len = k_cache.shape[1]
    inv_root = HEAD_DIM ** (-0.5)
    queries = q_new.reshape(rows_dev, kv_local, group_size, HEAD_DIM)
    cache_keys = k_cache.reshape(rows_dev, cache_len, kv_local, HEAD_DIM)
    cache_values = v_cache.reshape(rows_dev, cache_len, kv_local, HEAD_DIM)
    own_keys = k_new.reshape(rows_dev, kv_local, HEAD_DIM)
    own_values = v_new.reshape(rows_dev, kv_local, HEAD_DIM).astype(F32)
    cache_scores = (
        jnp.einsum("rkgd,rckd->rkgc", queries, cache_keys, preferred_element_type=F32) * inv_root
    )
    own_scores = (
        jnp.einsum("rkgd,rkd->rkg", queries, own_keys, preferred_element_type=F32) * inv_root
    )
    live_mask = (jnp.arange(cache_len, dtype=jnp.int32)[None, :] < lengths[:, None])[
        :, None, None, :
    ]
    cache_scores = jnp.where(live_mask, cache_scores, -1e30)
    peak = jnp.maximum(jnp.max(cache_scores, axis=3), own_scores)
    cache_exp = jnp.exp(cache_scores - peak[..., None])
    own_exp = jnp.exp(own_scores - peak)
    denominator = jnp.sum(cache_exp, axis=3) + own_exp
    cache_weights = (cache_exp / denominator[..., None]).astype(BF16)
    own_weights = (own_exp / denominator).astype(BF16).astype(F32)
    mixed_heads = jnp.einsum(
        "rkgc,rckd->rkgd", cache_weights, cache_values, preferred_element_type=F32
    )
    mixed_heads = mixed_heads + own_weights[..., None] * own_values[:, :, None, :]
    return mixed_heads.reshape(rows_dev, heads_local * HEAD_DIM).astype(BF16)


def ranks_of(member):
    n = member.shape[0]
    lower = (
        lax.broadcasted_iota(jnp.int32, (n, n), 0) >= lax.broadcasted_iota(jnp.int32, (n, n), 1)
    ).astype(BF16)
    counts = jnp.dot(lower, member.astype(BF16), preferred_element_type=F32).astype(jnp.int32)
    return jnp.where(member, counts - 1, -1)


def shards(
    q_new,
    k_new,
    v_new,
    k_cache,
    v_cache,
    lengths,
    attn_out_weight,
    residual,
    norm_gain,
    router_weight,
    expert_ids,
    gate_weight,
    up_weight,
    down_weight,
):
    chip = lax.axis_index("dp")
    core = lax.axis_index("side")
    plane = lax.axis_index("tensor")
    pos = jnp.stack([chip // 4, chip % 4, core]).astype(jnp.int32)
    first_core = core == 0

    labels = jnp.arange(EXPERTS, dtype=jnp.int32)
    block_ids = lax.dynamic_slice_in_dim(expert_ids, plane * 128, 128, 0)
    member = jnp.any(block_ids[:, :, None] == labels, axis=1)
    ranks = ranks_of(member).T
    slots = jnp.arange(32, dtype=jnp.int32)
    pick_own = (ranks[:, None, :] - core * 32 == slots[:, None]).astype(BF16).reshape(256, 128)
    pick_other = (
        (ranks[:, None, :] - (1 - core) * 32 == slots[:, None]).astype(BF16).reshape(256, 128)
    )
    ids_by_block = expert_ids.reshape(8, 128, 2)
    named = jnp.any(ids_by_block == plane, axis=2)
    ranks_mine = ranks_of(named.T).T
    partner_ids = jnp.sum(ids_by_block, axis=2) - plane
    hits = ranks_mine[:, None, :] - core * 32 == slots[:, None]
    partner = jnp.sum(jnp.where(hits, partner_ids[:, None, :], 0), axis=2).reshape(256, 1)
    signs = (labels == plane).astype(F32) - (labels == partner).astype(F32)

    attention = attend(q_new, k_new, v_new, k_cache, v_cache, lengths)
    first, second = gather_xy(attention[:16], attention[16:])
    rows_own = jnp.stack(
        [jnp.concatenate(first, axis=0), jnp.concatenate(second, axis=0)]
    )
    rows_other = swap_cores(rows_own)
    head_sums = pl.pallas_call(
        outproj_kernel,
        in_specs=[pl.BlockSpec(memory_space=pltpu.SMEM)]
        + [pl.BlockSpec(memory_space=pltpu.VMEM)] * 3,
        out_specs=pl.BlockSpec(memory_space=pltpu.VMEM),
        out_shape=jax.ShapeDtypeStruct((1024, 192), BF16),
        compiler_params=pltpu.CompilerParams(vmem_limit_bytes=VMEM_LIMIT),
        name="out_projection",
    )(pos, rows_own, rows_other, attn_out_weight)
    heads_in = lax.all_to_all(
        head_sums.reshape(8, 128, 192), "tensor", split_axis=0, concat_axis=0, tiled=True
    )
    hidden = (jnp.sum(heads_in.astype(F32), axis=0) + residual.astype(F32)).astype(BF16)
    hidden_other = swap_cores(hidden)
    hidden_chip = jnp.where(
        first_core,
        jnp.concatenate([hidden, hidden_other], axis=1),
        jnp.concatenate([hidden_other, hidden], axis=1),
    )
    routed = jnp.dot(pick_own, hidden_chip, preferred_element_type=F32).astype(BF16)
    mine = lax.all_to_all(
        routed.reshape(8, 32, 384), "tensor", split_axis=0, concat_axis=0, tiled=True
    ).reshape(256, 384)

    first, second = gather_xy(mine[:128], mine[128:])
    normed = pl.pallas_call(
        norm_kernel,
        in_specs=[pl.BlockSpec(memory_space=pltpu.SMEM)]
        + [pl.BlockSpec(memory_space=pltpu.VMEM)] * 9,
        out_specs=pl.BlockSpec(memory_space=pltpu.VMEM),
        out_shape=jax.ShapeDtypeStruct((16, 256, 384), BF16),
        compiler_params=pltpu.CompilerParams(vmem_limit_bytes=VMEM_LIMIT),
        name="norm",
    )(pos, *first, *second, norm_gain.reshape(16, 1, 384))
    normed_other = swap_cores(normed)
    gate_w, up_w, down_w = gate_weight[0], up_weight[0], down_weight[0]
    inner_own, logits = expert_call(normed, gate_w, up_w, router_weight)
    inner_other, _ = expert_call(normed_other, gate_w, up_w, router_weight)
    shares = jax.nn.sigmoid(jnp.sum(logits * signs, axis=1, keepdims=True))
    other_a, other_b = down_call(pos, inner_other, down_w)
    in_a, in_b = swap_cores(other_a), swap_cores(other_b)
    own_a, own_b = down_call(pos, inner_own, down_w)

    def add(*terms):
        total = terms[0].astype(F32)
        for term in terms[1:]:
            total = total + term.astype(F32)
        return total

    part_a = [add(own_a[d], in_a[d]) for d in range(4)]
    part_b = [add(own_b[d], in_b[d]) for d in range(4)]
    got_a = [lax.ppermute(part_a[d].astype(BF16), "dp", SHIFT_Y[d]) for d in (1, 2, 3)]
    got_b = [lax.ppermute(part_b[d].astype(BF16), "dp", SHIFT_X[d]) for d in (1, 2, 3)]
    row_a = add(part_a[0], *got_a)
    row_b = add(part_b[0], *got_b)
    got_a = [lax.ppermute(row_a[d].astype(BF16), "dp", SHIFT_X[d]) for d in (1, 2, 3)]
    got_b = [lax.ppermute(row_b[d].astype(BF16), "dp", SHIFT_Y[d]) for d in (1, 2, 3)]
    expert_out = jnp.concatenate([add(row_a[0], *got_a), add(row_b[0], *got_b)], axis=0)

    parts = (shares * expert_out).astype(BF16)
    back = lax.all_to_all(
        parts.reshape(8, 32, 384), "tensor", split_axis=0, concat_axis=0, tiled=True
    ).reshape(256, 384)
    keep = jnp.where(first_core, back[:, :192], back[:, 192:])
    give = jnp.where(first_core, back[:, 192:], back[:, :192])
    taken = swap_cores(give)

    def spread(pick, rows):
        return lax.dot_general(
            pick, rows, (((0,), (0,)), ((), ())), preferred_element_type=F32
        )

    return (
        hidden.astype(F32) + spread(pick_own, keep) + spread(pick_other, taken)
    ).astype(BF16)


def solution(mesh):
    return jax.shard_map(
        shards,
        mesh=mesh,
        in_specs=(
            P(("dp", "side"), "tensor"),
            P(("dp", "side"), "tensor"),
            P(("dp", "side"), "tensor"),
            P(("dp", "side"), None, "tensor"),
            P(("dp", "side"), None, "tensor"),
            P(("dp", "side")),
            P("tensor", ("dp", "side")),
            P("tensor", ("dp", "side")),
            P(),
            P(),
            P(),
            P("tensor", None, ("dp", "side")),
            P("tensor", None, ("dp", "side")),
            P("tensor", ("dp", "side"), None),
        ),
        out_specs=P("tensor", ("dp", "side")),
        check_vma=False,
    )
```

```python
import jax
import jax.numpy as jnp
from jax import lax
from jax.experimental import pallas as pl
from jax.experimental.pallas import tpu as pltpu
from jax.sharding import PartitionSpec as P

HEAD_DIM = 128
EXPERTS = 8
eps = 1e-05
F32 = jnp.float32
BF16 = jnp.bfloat16
VMEM_LIMIT = 48 * 1024 * 1024

SHIFT_X = [[(4 * x + y, 4 * ((x + d) % 4) + y) for x in range(4) for y in range(4)] for d in range(4)]
SHIFT_Y = [[(4 * x + y, 4 * x + (y + d) % 4) for x in range(4) for y in range(4)] for d in range(4)]
SWAP = [(0, 1), (1, 0)]


def swap_cores(a):
    return lax.ppermute(a, "side", SWAP)


def chip_at(pos, dx, dy):
    return ((pos[0] + dx) & 3) * 4 + ((pos[1] + dy) & 3)


def outproj_kernel(pos, g0, g1, g2, g3, w, out):
    for dy, ref in enumerate((g0, g1, g2, g3)):
        sums = jnp.dot(ref[...].reshape(128, 768), w[...], preferred_element_type=F32).astype(BF16)
        for dx in range(4):
            chip = chip_at(pos, -dx, -dy)
            row = pl.multiple_of((chip & 1) * 32, 32)
            out[chip // 2, pl.ds(row, 32), :] = sums[dx * 32 : dx * 32 + 32]


def expert_in_kernel(shift, first, last):
    def kernel(*refs):
        pos, own_a, own_b, other_a, other_b, gain, router, gate_w, up_w = refs[:9]
        rest = refs[9:]
        if not first:
            acc_in, logit_in, square_in = rest[:3]
            rest = rest[3:]
        if last:
            inner, logits = rest[:2]
            acc, logit, square = rest[2:5]
            w, sems = rest[5:]
        else:
            acc, logit, square = rest[:3]
            w, sems = rest[3:]

        def chip_of(h, i):
            return chip_at(pos, -i, -shift) if h == 0 else chip_at(pos, -shift, -i)

        def copies(h, i):
            rows = pl.ds(pl.multiple_of(chip_of(h, i) * 384, 128), 384)
            n = h * 4 + i
            return (
                pltpu.make_async_copy(gate_w.at[rows, :], w.at[n, :, 0:256], sems.at[n, 0]),
                pltpu.make_async_copy(up_w.at[rows, :], w.at[n, :, 256:512], sems.at[n, 1]),
            )

        def issue(n, _):
            for h in range(2):
                for copy in copies(h, n):
                    copy.start()
            return 0

        lax.fori_loop(0, 4, issue, 0)
        for h, own, other in ((0, own_a, other_a), (1, own_b, other_b)):
            if first:
                acc[h] = jnp.zeros((256, 512), F32)
                logit[h] = jnp.zeros((256, EXPERTS), F32)
                square[h] = jnp.zeros((256, 1), F32)
            else:
                acc[h] = acc_in[h]
                logit[h] = logit_in[h]
                square[h] = square_in[h]

            def add(i, _, h=h, own=own, other=other):
                chip = chip_of(h, i)
                v = jnp.concatenate([own[i], other[i]], axis=0).astype(F32)
                square[h] += jnp.sum(v * v, axis=1, keepdims=True)
                scaled = (v * gain[chip]).astype(BF16)
                for copy in copies(h, i):
                    copy.wait()
                acc[h] += jnp.dot(scaled, w[h * 4 + i], preferred_element_type=F32)
                logit[h] += jnp.dot(scaled, router[chip], preferred_element_type=F32)
                return 0

            lax.fori_loop(0, 4, add, 0)
            if last:
                scale = lax.rsqrt(square[h] * (1.0 / 6144.0) + eps)
                gate = acc[h, :, 0:256] * scale
                up = acc[h, :, 256:512] * scale
                inner[h] = (gate / (1.0 + jnp.exp(-gate)) * up).astype(BF16)
                logits[h] = logit[h] * scale

    return kernel


def expert_in_call(shift, pos, pieces, gain, router, gate_w, up_w, sums, last):
    vmem = pl.BlockSpec(memory_space=pltpu.VMEM)
    first = sums is None
    state = [
        ((2, 256, 512), F32),
        ((2, 256, EXPERTS), F32),
        ((2, 256, 1), F32),
    ]
    final = [((2, 256, 256), BF16), ((2, 256, EXPERTS), F32)]
    outs = final if last else state
    scratch = [pltpu.VMEM(*s) for s in state] if last else []
    return pl.pallas_call(
        expert_in_kernel(shift, first, last),
        in_specs=[pl.BlockSpec(memory_space=pltpu.SMEM)]
        + [vmem] * 6
        + [pl.BlockSpec(memory_space=pl.ANY)] * 2
        + [vmem] * (0 if first else 3),
        out_specs=[vmem] * len(outs),
        out_shape=[jax.ShapeDtypeStruct(*s) for s in outs],
        scratch_shapes=scratch
        + [pltpu.VMEM((8, 384, 512), BF16), pltpu.SemaphoreType.DMA((8, 2))],
        compiler_params=pltpu.CompilerParams(vmem_limit_bytes=VMEM_LIMIT),
        name="expert_in",
    )(pos, *pieces, gain, router, gate_w, up_w, *(() if first else sums))


def down_kernel(shift):
    def kernel(pos, inner, down_w, own, other, w, sems):
        def copy(h, i):
            chip = chip_at(pos, i, shift) if h == 0 else chip_at(pos, shift, i)
            columns = pl.ds(pl.multiple_of(chip * 384, 128), 384)
            n = h * 4 + i
            return pltpu.make_async_copy(down_w.at[:, columns], w.at[n], sems.at[n])

        def issue(i, _):
            for h in range(2):
                copy(h, i).start()
            return 0

        lax.fori_loop(0, 4, issue, 0)
        for h in range(2):

            def work(i, _, h=h):
                copy(h, i).wait()
                sums = jnp.dot(inner[h], w[h * 4 + i], preferred_element_type=F32).astype(BF16)
                own[h, i] = sums[:128]
                other[h, i] = sums[128:]
                return 0

            lax.fori_loop(0, 4, work, 0)

    return kernel


def down_call(shift, pos, inner, down_w):
    vmem = pl.BlockSpec(memory_space=pltpu.VMEM)
    return pl.pallas_call(
        down_kernel(shift),
        in_specs=[pl.BlockSpec(memory_space=pltpu.SMEM), vmem, pl.BlockSpec(memory_space=pl.ANY)],
        out_specs=[vmem, vmem],
        out_shape=[jax.ShapeDtypeStruct((2, 4, 128, 384), BF16)] * 2,
        scratch_shapes=[pltpu.VMEM((8, 256, 384), BF16), pltpu.SemaphoreType.DMA((8,))],
        compiler_params=pltpu.CompilerParams(vmem_limit_bytes=VMEM_LIMIT),
        name="expert_down",
    )(pos, inner, down_w)


def attend(q_new, k_new, v_new, k_cache, v_cache, lengths):
    rows_dev = q_new.shape[0]
    kv_local = k_new.shape[1] // HEAD_DIM
    heads_local = q_new.shape[1] // HEAD_DIM
    group_size = heads_local // kv_local
    cache_len = k_cache.shape[1]
    inv_root = HEAD_DIM ** (-0.5)
    queries = q_new.reshape(rows_dev, kv_local, group_size, HEAD_DIM)
    cache_keys = k_cache.reshape(rows_dev, cache_len, kv_local, HEAD_DIM)
    cache_values = v_cache.reshape(rows_dev, cache_len, kv_local, HEAD_DIM)
    own_keys = k_new.reshape(rows_dev, kv_local, HEAD_DIM)
    own_values = v_new.reshape(rows_dev, kv_local, HEAD_DIM).astype(F32)
    cache_scores = (
        jnp.einsum("rkgd,rckd->rkgc", queries, cache_keys, preferred_element_type=F32) * inv_root
    )
    own_scores = (
        jnp.einsum("rkgd,rkd->rkg", queries, own_keys, preferred_element_type=F32) * inv_root
    )
    live_mask = (jnp.arange(cache_len, dtype=jnp.int32)[None, :] < lengths[:, None])[
        :, None, None, :
    ]
    cache_scores = jnp.where(live_mask, cache_scores, -1e30)
    peak = jnp.maximum(jnp.max(cache_scores, axis=3), own_scores)
    cache_exp = jnp.exp(cache_scores - peak[..., None])
    own_exp = jnp.exp(own_scores - peak)
    denominator = jnp.sum(cache_exp, axis=3) + own_exp
    cache_weights = (cache_exp / denominator[..., None]).astype(BF16)
    own_weights = (own_exp / denominator).astype(BF16).astype(F32)
    mixed_heads = jnp.einsum(
        "rkgc,rckd->rkgd", cache_weights, cache_values, preferred_element_type=F32
    )
    mixed_heads = mixed_heads + own_weights[..., None] * own_values[:, :, None, :]
    return mixed_heads.reshape(rows_dev, heads_local * HEAD_DIM).astype(BF16)


def ranks_of(member):
    n = member.shape[0]
    lower = (
        lax.broadcasted_iota(jnp.int32, (n, n), 0) >= lax.broadcasted_iota(jnp.int32, (n, n), 1)
    ).astype(BF16)
    counts = jnp.dot(lower, member.astype(BF16), preferred_element_type=F32).astype(jnp.int32)
    return jnp.where(member, counts - 1, -1)


def shards(
    q_new,
    k_new,
    v_new,
    k_cache,
    v_cache,
    lengths,
    attn_out_weight,
    residual,
    norm_gain,
    router_weight,
    expert_ids,
    gate_weight,
    up_weight,
    down_weight,
):
    chip = lax.axis_index("dp")
    core = lax.axis_index("side")
    plane = lax.axis_index("tensor")
    pos = jnp.stack([chip // 4, chip % 4, core]).astype(jnp.int32)
    first_core = core == 0

    def by_core(own, other, axis):
        return jnp.where(
            first_core,
            jnp.concatenate([own, other], axis=axis),
            jnp.concatenate([other, own], axis=axis),
        )

    def half(a):
        return jnp.where(first_core, a[:, :192], a[:, 192:])

    out_w = by_core(attn_out_weight, swap_cores(attn_out_weight), 1)
    residual_chip = by_core(residual, swap_cores(residual), 1).reshape(2, 2, 32, 384)
    residual_half = jnp.where(first_core, residual_chip[:, 0], residual_chip[:, 1])

    labels = jnp.arange(EXPERTS, dtype=jnp.int32)
    block_ids = lax.dynamic_slice_in_dim(expert_ids, plane * 128, 128, 0)
    member = jnp.any(block_ids[:, :, None] == labels, axis=1)
    ranks = ranks_of(member).T
    ranks_by_core = ranks.reshape(8, 2, 2, 32).transpose(0, 2, 1, 3).reshape(8, 128)
    slots = jnp.arange(32, dtype=jnp.int32)

    def pick(ranks, side):
        return (ranks[:, None, :] - side * 32 == slots[:, None]).astype(BF16).reshape(256, 128)

    pick_routed = pick(ranks_by_core, core)
    pick_own, pick_other = pick(ranks, core), pick(ranks, 1 - core)
    ids_by_block = expert_ids.reshape(8, 128, 2)
    named = jnp.any(ids_by_block == plane, axis=2)
    ranks_mine = ranks_of(named.T).T
    partner_ids = jnp.sum(ids_by_block, axis=2) - plane
    hits = ranks_mine[:, None, :] - core * 32 == slots[:, None]
    partner = jnp.sum(jnp.where(hits, partner_ids[:, None, :], 0), axis=2).reshape(256, 1)
    signs = (labels == plane).astype(F32) - (labels == partner).astype(F32)

    attention = attend(q_new, k_new, v_new, k_cache, v_cache, lengths)
    rows_x = [lax.ppermute(attention, "dp", SHIFT_X[d]) for d in (1, 2, 3)]
    rows_x = jnp.stack([attention] + rows_x)
    rows_xy = [rows_x] + [lax.ppermute(rows_x, "dp", SHIFT_Y[d]) for d in (1, 2, 3)]
    vmem = pl.BlockSpec(memory_space=pltpu.VMEM)
    head_sums = pl.pallas_call(
        outproj_kernel,
        in_specs=[pl.BlockSpec(memory_space=pltpu.SMEM)] + [vmem] * 5,
        out_specs=vmem,
        out_shape=jax.ShapeDtypeStruct((8, 64, 384), BF16),
        compiler_params=pltpu.CompilerParams(vmem_limit_bytes=VMEM_LIMIT),
        name="out_projection",
    )(pos, *rows_xy, out_w)
    heads_in = lax.all_to_all(head_sums, "tensor", split_axis=0, concat_axis=0, tiled=True)
    hidden = (
        jnp.sum(heads_in.astype(F32), axis=0) + residual_half.reshape(64, 384).astype(F32)
    ).astype(BF16)
    hidden_chip = by_core(hidden, swap_cores(hidden), 0)
    hidden_rows = half(
        hidden_chip.reshape(2, 2, 32, 384).transpose(1, 0, 2, 3).reshape(128, 384)
    )
    routed = jnp.dot(pick_routed, hidden_chip, preferred_element_type=F32).astype(BF16)
    mine = lax.all_to_all(
        routed.reshape(8, 32, 384), "tensor", split_axis=0, concat_axis=0, tiled=True
    ).reshape(256, 384)

    a, b = mine[:128], mine[128:]
    got = lax.optimization_barrier(
        [lax.ppermute(a, "dp", SHIFT_X[d]) for d in (1, 2, 3)]
        + [lax.ppermute(b, "dp", SHIFT_Y[d]) for d in (1, 2, 3)]
    )
    stack_a, stack_b = jnp.stack([a] + got[:3]), jnp.stack([b] + got[3:])
    gain = norm_gain.reshape(16, 1, 384)
    router = router_weight.reshape(16, 384, EXPERTS)
    gate_w, up_w, down_w = gate_weight[0], up_weight[0], down_weight[0]
    near = {
        d: (lax.ppermute(stack_a, "dp", SHIFT_Y[d]), lax.ppermute(stack_b, "dp", SHIFT_X[d]))
        for d in (1, 3)
    }

    def take_in(shift, pair, sums, last=False):
        pieces = (*pair, swap_cores(pair[0]), swap_cores(pair[1]))
        return expert_in_call(shift, pos, pieces, gain, router, gate_w, up_w, sums, last)

    sums = take_in(0, (stack_a, stack_b), None)
    far_a, far_b, *sums = lax.optimization_barrier((stack_a, stack_b, *sums))
    far = lax.ppermute(far_a, "dp", SHIFT_Y[2]), lax.ppermute(far_b, "dp", SHIFT_X[2])
    sums = take_in(1, near[1], sums)
    sums = take_in(3, near[3], sums)
    inner, logits = take_in(2, far, sums, last=True)
    logits = logits[:, :128].reshape(256, EXPERTS)
    shares = jax.nn.sigmoid(jnp.sum(logits * signs, axis=1, keepdims=True))

    def add(*terms):
        total = terms[0].astype(F32)
        for term in terms[1:]:
            total = total + term.astype(F32)
        return total

    got_a, got_b = [], []
    for shift in (2, 1, 3, 0):
        own, other = down_call(shift, pos, inner, down_w)
        if shift:
            inner, other = lax.optimization_barrier((inner, other))
        other = swap_cores(other)
        part_a, part_b = add(own[0], other[0]), add(own[1], other[1])
        if shift:
            got_a.append(lax.ppermute(part_a.astype(BF16), "dp", SHIFT_Y[shift]))
            got_b.append(lax.ppermute(part_b.astype(BF16), "dp", SHIFT_X[shift]))
    row_a, row_b = add(part_a, *got_a), add(part_b, *got_b)
    got = lax.optimization_barrier(
        [lax.ppermute(row_a[d].astype(BF16), "dp", SHIFT_X[d]) for d in (1, 2, 3)]
        + [lax.ppermute(row_b[d].astype(BF16), "dp", SHIFT_Y[d]) for d in (1, 2, 3)]
    )
    expert_out = jnp.concatenate([add(row_a[0], *got[:3]), add(row_b[0], *got[3:])], axis=0)

    parts = (shares * expert_out).astype(BF16)
    back = lax.all_to_all(
        parts.reshape(8, 32, 384), "tensor", split_axis=0, concat_axis=0, tiled=True
    ).reshape(256, 384)
    keep = half(back)
    taken = swap_cores(jnp.where(first_core, back[:, 192:], back[:, :192]))

    def spread(pick, rows):
        return lax.dot_general(pick, rows, (((0,), (0,)), ((), ())), preferred_element_type=F32)

    return (hidden_rows.astype(F32) + spread(pick_own, keep) + spread(pick_other, taken)).astype(
        BF16
    )


def solution(mesh):
    return jax.shard_map(
        shards,
        mesh=mesh,
        in_specs=(
            P(("dp", "side"), "tensor"),
            P(("dp", "side"), "tensor"),
            P(("dp", "side"), "tensor"),
            P(("dp", "side"), None, "tensor"),
            P(("dp", "side"), None, "tensor"),
            P(("dp", "side")),
            P("tensor", ("dp", "side")),
            P("tensor", ("dp", "side")),
            P(),
            P(),
            P(),
            P("tensor", None, ("dp", "side")),
            P("tensor", None, ("dp", "side")),
            P("tensor", ("dp", "side"), None),
        ),
        out_specs=P("tensor", ("dp", "side")),
        check_vma=False,
    )
```

```python
import jax
import jax.numpy as jnp
from jax import lax
from jax.experimental import pallas as pl
from jax.experimental.pallas import tpu as pltpu
from jax.sharding import PartitionSpec as P

HEAD_DIM = 128
EXPERTS = 8
eps = 1e-05
F32 = jnp.float32
BF16 = jnp.bfloat16
VMEM_LIMIT = 48 * 1024 * 1024

SHIFT_X = [[(4 * x + y, 4 * ((x + d) % 4) + y) for x in range(4) for y in range(4)] for d in range(4)]
SHIFT_Y = [[(4 * x + y, 4 * x + (y + d) % 4) for x in range(4) for y in range(4)] for d in range(4)]
SWAP = [(0, 1), (1, 0)]


def swap_cores(a):
    return lax.ppermute(a, "side", SWAP)


def chip_at(pos, dx, dy):
    return ((pos[0] + dx) & 3) * 4 + ((pos[1] + dy) & 3)


def outproj_kernel(pos, g0, g1, g2, g3, w, out):
    for dy, ref in enumerate((g0, g1, g2, g3)):
        sums = jnp.dot(ref[...].reshape(128, 768), w[...], preferred_element_type=F32).astype(BF16)
        for dx in range(4):
            chip = chip_at(pos, -dx, -dy)
            row = pl.multiple_of((chip & 1) * 32, 32)
            out[chip // 2, pl.ds(row, 32), :] = sums[dx * 32 : dx * 32 + 32]


def norm_kernel(pos, a0, a1, a2, a3, b0, b1, b2, b3, gain, out):
    for h, refs in ((0, (a0, a1, a2, a3)), (1, (b0, b1, b2, b3))):

        def rows_of(n, _, h=h, refs=refs):
            rows = pl.ds(pl.multiple_of(n * 32, 32), 32)
            squares = jnp.zeros((32, 384), F32)
            for i in range(4):
                for j in range(4):
                    v = refs[i][j, rows, :].astype(F32)
                    squares = squares + v * v
            mean = jnp.sum(squares, axis=1, keepdims=True) * (1.0 / 6144.0)
            scale = lax.rsqrt(mean + eps)
            to = pl.ds(pl.multiple_of(h * 128 + n * 32, 32), 32)
            for i in range(4):
                for j in range(4):
                    chip = chip_at(pos, -j, -i) if h == 0 else chip_at(pos, -i, -j)
                    columns = pl.ds(pl.multiple_of(chip * 384, 128), 384)
                    v = refs[i][j, rows, :].astype(F32)
                    out[to, columns] = (v * scale * gain[chip]).astype(BF16)
            return 0

        lax.fori_loop(0, 4, rows_of, 0)


def down_kernel(pos, inner, down_w, near, far, w, sems):
    def copy(dx, dy):
        columns = pl.ds(pl.multiple_of(chip_at(pos, dx, dy) * 384, 128), 384)
        n = dx * 4 + dy
        return pltpu.make_async_copy(down_w.at[:, columns], w.at[n], sems.at[n])

    def issue(n, _):
        copy(n // 4, n % 4).start()
        return 0

    def arrive(n, _):
        copy(n // 4, n % 4).wait()
        return 0

    lax.fori_loop(0, 16, issue, 0)
    lax.fori_loop(0, 16, arrive, 0)
    for out, base, step in ((near, 1, 2), (far, 2, -2)):

        def work(n, _, out=out, base=base, step=step):
            k, i = n // 4, n % 4
            shift = base + step * k
            first = jnp.dot(inner[0:128, :], w[i * 4 + shift], preferred_element_type=F32)
            second = jnp.dot(inner[128:256, :], w[shift * 4 + i], preferred_element_type=F32)
            out[k, 0, i] = first.astype(BF16)
            out[k, 1, i] = second.astype(BF16)
            return 0

        lax.fori_loop(0, 8, work, 0)


def down_call(pos, inner, down_w):
    vmem = pl.BlockSpec(memory_space=pltpu.VMEM)
    return pl.pallas_call(
        down_kernel,
        in_specs=[pl.BlockSpec(memory_space=pltpu.SMEM), vmem, pl.BlockSpec(memory_space=pl.ANY)],
        out_specs=[vmem, vmem],
        out_shape=[jax.ShapeDtypeStruct((2, 2, 4, 128, 384), BF16)] * 2,
        scratch_shapes=[pltpu.VMEM((16, 256, 384), BF16), pltpu.SemaphoreType.DMA((16,))],
        compiler_params=pltpu.CompilerParams(vmem_limit_bytes=VMEM_LIMIT),
        name="expert_down",
    )(pos, inner, down_w)


def attend(q_new, k_new, v_new, k_cache, v_cache, lengths):
    rows_dev = q_new.shape[0]
    kv_local = k_new.shape[1] // HEAD_DIM
    heads_local = q_new.shape[1] // HEAD_DIM
    group_size = heads_local // kv_local
    cache_len = k_cache.shape[1]
    inv_root = HEAD_DIM ** (-0.5)
    queries = q_new.reshape(rows_dev, kv_local, group_size, HEAD_DIM)
    cache_keys = k_cache.reshape(rows_dev, cache_len, kv_local, HEAD_DIM)
    cache_values = v_cache.reshape(rows_dev, cache_len, kv_local, HEAD_DIM)
    own_keys = k_new.reshape(rows_dev, kv_local, HEAD_DIM)
    own_values = v_new.reshape(rows_dev, kv_local, HEAD_DIM).astype(F32)
    cache_scores = (
        jnp.einsum("rkgd,rckd->rkgc", queries, cache_keys, preferred_element_type=F32) * inv_root
    )
    own_scores = (
        jnp.einsum("rkgd,rkd->rkg", queries, own_keys, preferred_element_type=F32) * inv_root
    )
    live_mask = (jnp.arange(cache_len, dtype=jnp.int32)[None, :] < lengths[:, None])[
        :, None, None, :
    ]
    cache_scores = jnp.where(live_mask, cache_scores, -1e30)
    peak = jnp.maximum(jnp.max(cache_scores, axis=3), own_scores)
    cache_exp = jnp.exp(cache_scores - peak[..., None])
    own_exp = jnp.exp(own_scores - peak)
    denominator = jnp.sum(cache_exp, axis=3) + own_exp
    cache_weights = (cache_exp / denominator[..., None]).astype(BF16)
    own_weights = (own_exp / denominator).astype(BF16).astype(F32)
    mixed_heads = jnp.einsum(
        "rkgc,rckd->rkgd", cache_weights, cache_values, preferred_element_type=F32
    )
    mixed_heads = mixed_heads + own_weights[..., None] * own_values[:, :, None, :]
    return mixed_heads.reshape(rows_dev, heads_local * HEAD_DIM).astype(BF16)


def ranks_of(member):
    n = member.shape[0]
    lower = (
        lax.broadcasted_iota(jnp.int32, (n, n), 0) >= lax.broadcasted_iota(jnp.int32, (n, n), 1)
    ).astype(BF16)
    counts = jnp.dot(lower, member.astype(BF16), preferred_element_type=F32).astype(jnp.int32)
    return jnp.where(member, counts - 1, -1)


def shards(
    q_new,
    k_new,
    v_new,
    k_cache,
    v_cache,
    lengths,
    attn_out_weight,
    residual,
    norm_gain,
    router_weight,
    expert_ids,
    gate_weight,
    up_weight,
    down_weight,
):
    chip = lax.axis_index("dp")
    core = lax.axis_index("side")
    plane = lax.axis_index("tensor")
    pos = jnp.stack([chip // 4, chip % 4, core]).astype(jnp.int32)
    first_core = core == 0

    def by_core(own, other, axis):
        return jnp.where(
            first_core,
            jnp.concatenate([own, other], axis=axis),
            jnp.concatenate([other, own], axis=axis),
        )

    def half(a):
        return jnp.where(first_core, a[:, :192], a[:, 192:])

    attention = attend(q_new, k_new, v_new, k_cache, v_cache, lengths)
    labels = jnp.arange(EXPERTS, dtype=jnp.int32)
    block_ids = lax.dynamic_slice_in_dim(expert_ids, plane * 128, 128, 0)
    member = jnp.any(block_ids[:, :, None] == labels, axis=1)
    ranks = ranks_of(member).T
    ranks_by_core = ranks.reshape(8, 2, 2, 32).transpose(0, 2, 1, 3).reshape(8, 128)
    slots = jnp.arange(32, dtype=jnp.int32)

    def pick(ranks, side):
        return (ranks[:, None, :] - side * 32 == slots[:, None]).astype(BF16).reshape(256, 128)

    pick_routed = pick(ranks_by_core, core)
    pick_own, pick_other = pick(ranks, core), pick(ranks, 1 - core)
    ids_by_block = expert_ids.reshape(8, 128, 2)
    named = jnp.any(ids_by_block == plane, axis=2)
    ranks_mine = ranks_of(named.T).T
    partner_ids = jnp.sum(ids_by_block, axis=2) - plane
    hits = ranks_mine[:, None, :] - core * 32 == slots[:, None]
    partner = jnp.sum(jnp.where(hits, partner_ids[:, None, :], 0), axis=2).reshape(256, 1)
    signs = (labels == plane).astype(F32) - (labels == partner).astype(F32)

    rows_x = [lax.ppermute(attention, "dp", SHIFT_X[d]) for d in (1, 2, 3)]
    rows_x = jnp.stack([attention] + rows_x)
    columns, rows_x = lax.optimization_barrier(
        (jnp.concatenate([attn_out_weight, residual], axis=0), rows_x)
    )
    columns = by_core(columns, swap_cores(columns), 1)
    out_w = columns[:768]
    residual_chip = columns[768:].reshape(2, 2, 32, 384)
    residual_half = jnp.where(first_core, residual_chip[:, 0], residual_chip[:, 1])
    rows_xy = [rows_x] + [lax.ppermute(rows_x, "dp", SHIFT_Y[d]) for d in (1, 2, 3)]
    vmem = pl.BlockSpec(memory_space=pltpu.VMEM)
    head_sums = pl.pallas_call(
        outproj_kernel,
        in_specs=[pl.BlockSpec(memory_space=pltpu.SMEM)] + [vmem] * 5,
        out_specs=vmem,
        out_shape=jax.ShapeDtypeStruct((8, 64, 384), BF16),
        compiler_params=pltpu.CompilerParams(vmem_limit_bytes=VMEM_LIMIT),
        name="out_projection",
    )(pos, *rows_xy, out_w)
    heads_in = lax.all_to_all(head_sums, "tensor", split_axis=0, concat_axis=0, tiled=True)
    hidden = (
        jnp.sum(heads_in.astype(F32), axis=0) + residual_half.reshape(64, 384).astype(F32)
    ).astype(BF16)
    hidden_chip = by_core(hidden, swap_cores(hidden), 0)
    hidden_rows = half(
        hidden_chip.reshape(2, 2, 32, 384).transpose(1, 0, 2, 3).reshape(128, 384)
    )
    routed = jnp.dot(pick_routed, hidden_chip, preferred_element_type=F32).astype(BF16)
    mine = lax.all_to_all(
        routed.reshape(8, 32, 384), "tensor", split_axis=0, concat_axis=0, tiled=True
    ).reshape(256, 384)

    a, b = mine[:128], mine[128:]
    got = lax.optimization_barrier(
        [lax.ppermute(a, "dp", SHIFT_X[d]) for d in (1, 2, 3)]
        + [lax.ppermute(b, "dp", SHIFT_Y[d]) for d in (1, 2, 3)]
    )
    stack_a, stack_b = jnp.stack([a] + got[:3]), jnp.stack([b] + got[3:])
    gate_w, up_w, down_w = gate_weight[0], up_weight[0], down_weight[0]
    a1, a3, b1, b3 = [lax.ppermute(stack_a, "dp", SHIFT_Y[d]) for d in (1, 3)] + [
        lax.ppermute(stack_b, "dp", SHIFT_X[d]) for d in (1, 3)
    ]
    far_a, far_b, a1, b1 = lax.optimization_barrier((stack_a, stack_b, a1, b1))
    a2, b2 = lax.ppermute(far_a, "dp", SHIFT_Y[2]), lax.ppermute(far_b, "dp", SHIFT_X[2])
    normed = pl.pallas_call(
        norm_kernel,
        in_specs=[pl.BlockSpec(memory_space=pltpu.SMEM)] + [vmem] * 9,
        out_specs=vmem,
        out_shape=jax.ShapeDtypeStruct((256, 6144), BF16),
        compiler_params=pltpu.CompilerParams(vmem_limit_bytes=VMEM_LIMIT),
        name="norm",
    )(pos, stack_a, a1, a2, a3, stack_b, b1, b2, b3, norm_gain.reshape(16, 1, 384))
    normed_other = swap_cores(normed)

    def expert_in(rows):
        gate = jnp.dot(rows, gate_w, preferred_element_type=F32)
        up = jnp.dot(rows, up_w, preferred_element_type=F32)
        return (jax.nn.silu(gate) * up).astype(BF16)

    logits = jnp.dot(normed, router_weight, preferred_element_type=F32)
    shares = jax.nn.sigmoid(jnp.sum(logits * signs, axis=1, keepdims=True))
    own = down_call(pos, expert_in(normed), down_w)
    own, normed_other = lax.optimization_barrier((own, normed_other))
    other = down_call(pos, expert_in(normed_other), down_w)

    def add(*terms):
        total = terms[0].astype(F32)
        for term in terms[1:]:
            total = total + term.astype(F32)
        return total

    near = swap_cores(other[0])
    far = swap_cores(other[1])
    parts = [add(own[0][k, h], near[k, h]).astype(BF16) for k in (0, 1) for h in (0, 1)]
    far, *parts = lax.optimization_barrier((far, *parts))
    parts += [add(own[1][0, h], far[0, h]).astype(BF16) for h in (0, 1)]
    got_a = [lax.ppermute(parts[2 * n], "dp", SHIFT_Y[d]) for n, d in enumerate((1, 3, 2))]
    got_b = [lax.ppermute(parts[2 * n + 1], "dp", SHIFT_X[d]) for n, d in enumerate((1, 3, 2))]
    part_a, part_b = add(own[1][1, 0], far[1, 0]), add(own[1][1, 1], far[1, 1])
    row_a, row_b = add(part_a, *got_a), add(part_b, *got_b)
    got = lax.optimization_barrier(
        [lax.ppermute(row_a[d].astype(BF16), "dp", SHIFT_X[d]) for d in (1, 2, 3)]
        + [lax.ppermute(row_b[d].astype(BF16), "dp", SHIFT_Y[d]) for d in (1, 2, 3)]
    )
    expert_out = jnp.concatenate([add(row_a[0], *got[:3]), add(row_b[0], *got[3:])], axis=0)

    parts = (shares * expert_out).astype(BF16)
    back = lax.all_to_all(
        parts.reshape(8, 32, 384), "tensor", split_axis=0, concat_axis=0, tiled=True
    ).reshape(256, 384)
    keep = half(back)
    taken = swap_cores(jnp.where(first_core, back[:, 192:], back[:, :192]))

    def spread(pick, rows):
        return lax.dot_general(pick, rows, (((0,), (0,)), ((), ())), preferred_element_type=F32)

    return (hidden_rows.astype(F32) + spread(pick_own, keep) + spread(pick_other, taken)).astype(
        BF16
    )


def solution(mesh):
    return jax.shard_map(
        shards,
        mesh=mesh,
        in_specs=(
            P(("dp", "side"), "tensor"),
            P(("dp", "side"), "tensor"),
            P(("dp", "side"), "tensor"),
            P(("dp", "side"), None, "tensor"),
            P(("dp", "side"), None, "tensor"),
            P(("dp", "side")),
            P("tensor", ("dp", "side")),
            P("tensor", ("dp", "side")),
            P(),
            P(),
            P(),
            P("tensor", None, ("dp", "side")),
            P("tensor", None, ("dp", "side")),
            P("tensor", ("dp", "side"), None),
        ),
        out_specs=P("tensor", ("dp", "side")),
        check_vma=False,
    )
```

```python
import jax
import jax.numpy as jnp
from jax import lax
from jax.experimental import pallas as pl
from jax.experimental.pallas import tpu as pltpu
from jax.sharding import PartitionSpec as P

HEAD_DIM = 128
EXPERTS = 8
eps = 1e-05
F32 = jnp.float32
BF16 = jnp.bfloat16
VMEM_LIMIT = 16 * 1024 * 1024

SHIFT_X = [[(4 * x + y, 4 * ((x + d) % 4) + y) for x in range(4) for y in range(4)] for d in range(4)]
SHIFT_Y = [[(4 * x + y, 4 * x + (y + d) % 4) for x in range(4) for y in range(4)] for d in range(4)]
SWAP = [(0, 1), (1, 0)]


def swap_cores(a):
    return lax.ppermute(a, "side", SWAP)


def chip_at(pos, dx, dy):
    return ((pos[0] + dx) & 3) * 4 + ((pos[1] + dy) & 3)


def outproj_kernel(pos, g0, g1, g2, g3, w, out):
    for dy, ref in enumerate((g0, g1, g2, g3)):

        def work(dx, _, dy=dy, ref=ref):
            sums = jnp.dot(ref[dx], w[...], preferred_element_type=F32)
            chip = chip_at(pos, -dx, -dy)
            out[chip // 2, pl.ds(pl.multiple_of((chip & 1) * 32, 32), 32), :] = sums.astype(BF16)
            return 0

        lax.fori_loop(0, 4, work, 0)


def at_half(pos, h, i, shift):
    return chip_at(pos, i, shift) if h == 0 else chip_at(pos, shift, i)


def norm_kernel(pos, a0, a1, a2, a3, b0, b1, b2, b3, gain, out):
    for h, refs in ((0, (a0, a1, a2, a3)), (1, (b0, b1, b2, b3))):

        def rows_of(n, _, h=h, refs=refs):
            rows = pl.ds(pl.multiple_of(n * 32, 32), 32)
            to = pl.ds(pl.multiple_of(h * 128 + n * 32, 32), 32)

            def square(j, total):
                for i in range(4):
                    v = refs[i][j, rows, :].astype(F32)
                    total = total + v * v
                return total

            squares = lax.fori_loop(0, 4, square, jnp.zeros((32, 384), F32))
            mean = jnp.sum(squares, axis=1, keepdims=True) * (1.0 / 6144.0)
            scale = lax.rsqrt(mean + eps)

            def store(j, _):
                for i in range(4):
                    chip = at_half(pos, h, -j, -i)
                    columns = pl.ds(pl.multiple_of(chip * 384, 128), 384)
                    v = refs[i][j, rows, :].astype(F32)
                    out[to, columns] = (v * scale * gain[chip]).astype(BF16)
                return 0

            lax.fori_loop(0, 4, store, 0)
            return 0

        lax.fori_loop(0, 4, rows_of, 0)


def combine_kernel(h):
    def kernel(pos, own, other, *outs):
        def work(n, _):
            i, rows = n // 4, pl.ds(pl.multiple_of((n % 4) * 32, 32), 32)
            to = pl.ds(pl.multiple_of(h * 128 + (n % 4) * 32, 32), 32)
            for k in range(4):
                columns = pl.ds(pl.multiple_of(at_half(pos, h, i, k) * 384, 128), 384)
                mine = own[to, columns].astype(F32)
                total = mine + other[rows, columns].astype(F32)
                outs[k][i, rows, :] = total.astype(BF16)
            return 0

        lax.fori_loop(0, 16, work, 0)

    return kernel


def rows_kernel(mine, got1, got2, got3, *outs):
    def work(n, _):
        rows = pl.ds(pl.multiple_of(n * 32, 32), 32)
        for i in range(4):
            total = mine[i, rows, :].astype(F32)
            for got in (got1, got2, got3):
                total = total + got[i, rows, :].astype(F32)
            outs[i][rows, :] = total.astype(outs[i].dtype)
        return 0

    lax.fori_loop(0, 4, work, 0)


def local_call(kernel, outs, name, *args, smem=True):
    vmem = pl.BlockSpec(memory_space=pltpu.VMEM)
    first = [pl.BlockSpec(memory_space=pltpu.SMEM)] if smem else []
    return pl.pallas_call(
        kernel,
        in_specs=first + [vmem] * (len(args) - len(first)),
        out_specs=[vmem] * len(outs),
        out_shape=[jax.ShapeDtypeStruct(*o) for o in outs],
        compiler_params=pltpu.CompilerParams(vmem_limit_bytes=VMEM_LIMIT),
        name=name,
    )(*args)


def attend(q_new, k_new, v_new, k_cache, v_cache, lengths):
    rows_dev = q_new.shape[0]
    kv_local = k_new.shape[1] // HEAD_DIM
    heads_local = q_new.shape[1] // HEAD_DIM
    group_size = heads_local // kv_local
    cache_len = k_cache.shape[1]
    inv_root = HEAD_DIM ** (-0.5)
    queries = q_new.reshape(rows_dev, kv_local, group_size, HEAD_DIM)
    cache_keys = k_cache.reshape(rows_dev, cache_len, kv_local, HEAD_DIM)
    cache_values = v_cache.reshape(rows_dev, cache_len, kv_local, HEAD_DIM)
    own_keys = k_new.reshape(rows_dev, kv_local, HEAD_DIM)
    own_values = v_new.reshape(rows_dev, kv_local, HEAD_DIM).astype(F32)
    cache_scores = (
        jnp.einsum("rkgd,rckd->rkgc", queries, cache_keys, preferred_element_type=F32) * inv_root
    )
    own_scores = (
        jnp.einsum("rkgd,rkd->rkg", queries, own_keys, preferred_element_type=F32) * inv_root
    )
    live_mask = (jnp.arange(cache_len, dtype=jnp.int32)[None, :] < lengths[:, None])[
        :, None, None, :
    ]
    cache_scores = jnp.where(live_mask, cache_scores, -1e30)
    peak = jnp.maximum(jnp.max(cache_scores, axis=3), own_scores)
    cache_exp = jnp.exp(cache_scores - peak[..., None])
    own_exp = jnp.exp(own_scores - peak)
    denominator = jnp.sum(cache_exp, axis=3) + own_exp
    cache_weights = (cache_exp / denominator[..., None]).astype(BF16)
    own_weights = (own_exp / denominator).astype(BF16).astype(F32)
    mixed_heads = jnp.einsum(
        "rkgc,rckd->rkgd", cache_weights, cache_values, preferred_element_type=F32
    )
    mixed_heads = mixed_heads + own_weights[..., None] * own_values[:, :, None, :]
    return mixed_heads.reshape(rows_dev, heads_local * HEAD_DIM).astype(BF16)


def ranks_of(member):
    n = member.shape[0]
    lower = (
        lax.broadcasted_iota(jnp.int32, (n, n), 0) >= lax.broadcasted_iota(jnp.int32, (n, n), 1)
    ).astype(BF16)
    counts = jnp.dot(lower, member.astype(BF16), preferred_element_type=F32).astype(jnp.int32)
    return jnp.where(member, counts - 1, -1)


def shards(
    q_new,
    k_new,
    v_new,
    k_cache,
    v_cache,
    lengths,
    attn_out_weight,
    residual,
    norm_gain,
    router_weight,
    expert_ids,
    gate_weight,
    up_weight,
    down_weight,
):
    chip = lax.axis_index("dp")
    core = lax.axis_index("side")
    plane = lax.axis_index("tensor")
    pos = jnp.stack([chip // 4, chip % 4, core]).astype(jnp.int32)
    first_core = core == 0

    def by_core(own, other, axis):
        return jnp.where(
            first_core,
            jnp.concatenate([own, other], axis=axis),
            jnp.concatenate([other, own], axis=axis),
        )

    def half(a):
        return jnp.where(first_core, a[:, :192], a[:, 192:])

    attention = attend(q_new, k_new, v_new, k_cache, v_cache, lengths)
    out_w = by_core(attn_out_weight, swap_cores(attn_out_weight), 1)
    residual_chip = by_core(residual, swap_cores(residual), 1).reshape(2, 2, 32, 384)
    residual_half = jnp.where(first_core, residual_chip[:, 0], residual_chip[:, 1])

    labels = jnp.arange(EXPERTS, dtype=jnp.int32)
    block_ids = lax.dynamic_slice_in_dim(expert_ids, plane * 128, 128, 0)
    member = jnp.any(block_ids[:, :, None] == labels, axis=1)
    ranks = ranks_of(member).T
    ranks_by_core = ranks.reshape(8, 2, 2, 32).transpose(0, 2, 1, 3).reshape(8, 128)
    slots = jnp.arange(32, dtype=jnp.int32)

    def pick(ranks, side):
        return (ranks[:, None, :] - side * 32 == slots[:, None]).astype(BF16).reshape(256, 128)

    pick_routed = pick(ranks_by_core, core)
    pick_own, pick_other = pick(ranks, core), pick(ranks, 1 - core)
    ids_by_block = expert_ids.reshape(8, 128, 2)
    named = jnp.any(ids_by_block == plane, axis=2)
    ranks_mine = ranks_of(named.T).T
    partner_ids = jnp.sum(ids_by_block, axis=2) - plane
    hits = ranks_mine[:, None, :] - core * 32 == slots[:, None]
    partner = jnp.sum(jnp.where(hits, partner_ids[:, None, :], 0), axis=2).reshape(256, 1)
    signs = (labels == plane).astype(F32) - (labels == partner).astype(F32)

    rows_x = [lax.ppermute(attention, "dp", SHIFT_X[d]) for d in (1, 2, 3)]
    rows_x = jnp.stack([attention] + rows_x)
    rows_xy = [rows_x] + [lax.ppermute(rows_x, "dp", SHIFT_Y[d]) for d in (1, 2, 3)]
    vmem = pl.BlockSpec(memory_space=pltpu.VMEM)
    head_sums = pl.pallas_call(
        outproj_kernel,
        in_specs=[pl.BlockSpec(memory_space=pltpu.SMEM)] + [vmem] * 5,
        out_specs=vmem,
        out_shape=jax.ShapeDtypeStruct((8, 64, 384), BF16),
        compiler_params=pltpu.CompilerParams(vmem_limit_bytes=VMEM_LIMIT),
        name="out_projection",
    )(pos, *rows_xy, out_w)
    heads_in = lax.all_to_all(head_sums, "tensor", split_axis=0, concat_axis=0, tiled=True)
    hidden = (
        jnp.sum(heads_in.astype(F32), axis=0) + residual_half.reshape(64, 384).astype(F32)
    ).astype(BF16)
    hidden_chip = by_core(hidden, swap_cores(hidden), 0)
    hidden_rows = half(
        hidden_chip.reshape(2, 2, 32, 384).transpose(1, 0, 2, 3).reshape(128, 384)
    )
    routed = jnp.dot(pick_routed, hidden_chip, preferred_element_type=F32).astype(BF16)
    mine = lax.all_to_all(
        routed.reshape(8, 32, 384), "tensor", split_axis=0, concat_axis=0, tiled=True
    ).reshape(256, 384)

    a, b = mine[:128], mine[128:]
    got = lax.optimization_barrier(
        [lax.ppermute(a, "dp", SHIFT_X[d]) for d in (1, 2, 3)]
        + [lax.ppermute(b, "dp", SHIFT_Y[d]) for d in (1, 2, 3)]
    )
    stack_a, stack_b = jnp.stack([a] + got[:3]), jnp.stack([b] + got[3:])
    gate_w, up_w, down_w = gate_weight[0], up_weight[0], down_weight[0]
    a1, a3, b1, b3 = [lax.ppermute(stack_a, "dp", SHIFT_Y[d]) for d in (1, 3)] + [
        lax.ppermute(stack_b, "dp", SHIFT_X[d]) for d in (1, 3)
    ]
    far_a, far_b, a1, b1 = lax.optimization_barrier((stack_a, stack_b, a1, b1))
    a2, b2 = lax.ppermute(far_a, "dp", SHIFT_Y[2]), lax.ppermute(far_b, "dp", SHIFT_X[2])
    gain = norm_gain.reshape(16, 1, 384)
    normed = local_call(
        norm_kernel,
        [((256, 6144), BF16)],
        "norm",
        pos,
        *(stack_a, a1, a2, a3),
        *(stack_b, b1, b2, b3),
        gain,
    )[0]
    normed_other = swap_cores(normed)

    def expert_in(rows):
        gate = jnp.dot(rows, gate_w, preferred_element_type=F32)
        up = jnp.dot(rows, up_w, preferred_element_type=F32)
        return (jax.nn.silu(gate) * up).astype(BF16)

    def expert_out_of(rows):
        return jnp.dot(rows, down_w, preferred_element_type=F32).astype(BF16)

    logits = jnp.dot(normed, router_weight, preferred_element_type=F32)
    shares = jax.nn.sigmoid(jnp.sum(logits * signs, axis=1, keepdims=True))
    inner = expert_in(normed)
    inner, normed_other = lax.optimization_barrier((inner, normed_other))
    own = expert_out_of(inner)
    inner_other = expert_in(normed_other)
    other = [swap_cores(expert_out_of(inner_other[r : r + 128])) for r in (0, 128)]

    expert_out = []
    for h in (0, 1):
        near, far = (SHIFT_Y, SHIFT_X) if h == 0 else (SHIFT_X, SHIFT_Y)
        stack = (4, 128, 384)
        sums = local_call(
            combine_kernel(h),
            [(stack, BF16)] * 4,
            "combine_cores",
            pos,
            own,
            other[h],
        )
        got = [lax.ppermute(sums[d], "dp", near[d]) for d in (1, 3, 2)]
        rows = local_call(
            rows_kernel,
            [((128, 384), F32)] + [((128, 384), BF16)] * 3,
            "sum_rows",
            sums[0],
            *got,
            smem=False,
        )
        got = [lax.ppermute(rows[d], "dp", far[d]) for d in (1, 3, 2)]
        expert_out.append(rows[0] + sum(g.astype(F32) for g in got))
    expert_out = jnp.concatenate(expert_out)

    parts = (shares * expert_out).astype(BF16)
    back = lax.all_to_all(
        parts.reshape(8, 32, 384), "tensor", split_axis=0, concat_axis=0, tiled=True
    ).reshape(256, 384)
    keep = half(back)
    taken = swap_cores(jnp.where(first_core, back[:, 192:], back[:, :192]))

    def spread(pick, rows):
        return lax.dot_general(pick, rows, (((0,), (0,)), ((), ())), preferred_element_type=F32)

    return (hidden_rows.astype(F32) + spread(pick_own, keep) + spread(pick_other, taken)).astype(
        BF16
    )


def solution(mesh):
    return jax.shard_map(
        shards,
        mesh=mesh,
        in_specs=(
            P(("dp", "side"), "tensor"),
            P(("dp", "side"), "tensor"),
            P(("dp", "side"), "tensor"),
            P(("dp", "side"), None, "tensor"),
            P(("dp", "side"), None, "tensor"),
            P(("dp", "side")),
            P("tensor", ("dp", "side")),
            P("tensor", ("dp", "side")),
            P(),
            P(),
            P(),
            P("tensor", None, ("dp", "side")),
            P("tensor", None, ("dp", "side")),
            P("tensor", ("dp", "side"), None),
        ),
        out_specs=P("tensor", ("dp", "side")),
        check_vma=False,
    )
```

```python
import jax
import jax.numpy as jnp
from jax import lax
from jax.experimental import pallas as pl
from jax.experimental.pallas import tpu as pltpu
from jax.sharding import PartitionSpec as P

HEAD_DIM = 128
EXPERTS = 8
eps = 1e-05
F32 = jnp.float32
BF16 = jnp.bfloat16
VMEM_LIMIT = 16 * 1024 * 1024

SHIFT_X = [[(4 * x + y, 4 * ((x + d) % 4) + y) for x in range(4) for y in range(4)] for d in range(4)]
SHIFT_Y = [[(4 * x + y, 4 * x + (y + d) % 4) for x in range(4) for y in range(4)] for d in range(4)]
SWAP = [(0, 1), (1, 0)]


def swap_cores(a):
    return lax.ppermute(a, "side", SWAP)


def chip_at(pos, dx, dy):
    return ((pos[0] + dx) & 3) * 4 + ((pos[1] + dy) & 3)


def outproj_kernel(pos, g0, g1, g2, g3, w, out):
    for dy, ref in enumerate((g0, g1, g2, g3)):
        sums = jnp.dot(ref[...].reshape(128, 768), w[...], preferred_element_type=F32).astype(BF16)
        for dx in range(4):
            chip = chip_at(pos, -dx, -dy)
            row = pl.multiple_of((chip & 1) * 32, 32)
            out[chip // 2, pl.ds(row, 32), :] = sums[dx * 32 : dx * 32 + 32]


def at_half(pos, h, i, shift):
    return chip_at(pos, i, shift) if h == 0 else chip_at(pos, shift, i)


def norm_kernel(pos, a0, a1, a2, a3, b0, b1, b2, b3, gain, out):
    for h, refs in ((0, (a0, a1, a2, a3)), (1, (b0, b1, b2, b3))):

        def rows_of(n, _, h=h, refs=refs):
            rows = pl.ds(pl.multiple_of(n * 32, 32), 32)
            to = pl.ds(pl.multiple_of(h * 128 + n * 32, 32), 32)

            def square(j, total):
                for i in range(4):
                    v = refs[i][j, rows, :].astype(F32)
                    total = total + v * v
                return total

            squares = lax.fori_loop(0, 4, square, jnp.zeros((32, 384), F32))
            mean = jnp.sum(squares, axis=1, keepdims=True) * (1.0 / 6144.0)
            scale = lax.rsqrt(mean + eps)

            def store(j, _):
                for i in range(4):
                    chip = at_half(pos, h, -j, -i)
                    columns = pl.ds(pl.multiple_of(chip * 384, 128), 384)
                    v = refs[i][j, rows, :].astype(F32)
                    out[to, columns] = (v * scale * gain[chip]).astype(BF16)
                return 0

            lax.fori_loop(0, 4, store, 0)
            return 0

        lax.fori_loop(0, 4, rows_of, 0)


def combine_kernel(h):
    def kernel(pos, own, other, *outs):
        def work(n, _):
            i, rows = n // 4, pl.ds(pl.multiple_of((n % 4) * 32, 32), 32)
            to = pl.ds(pl.multiple_of(h * 128 + (n % 4) * 32, 32), 32)
            for k in range(4):
                columns = pl.ds(pl.multiple_of(at_half(pos, h, i, k) * 384, 128), 384)
                mine = own[to, columns].astype(F32)
                total = mine + other[rows, columns].astype(F32)
                outs[k][i, rows, :] = total.astype(BF16)
            return 0

        lax.fori_loop(0, 16, work, 0)

    return kernel


def rows_kernel(mine, got1, got2, got3, *outs):
    def work(n, _):
        rows = pl.ds(pl.multiple_of(n * 32, 32), 32)
        for i in range(4):
            total = mine[i, rows, :].astype(F32)
            for got in (got1, got2, got3):
                total = total + got[i, rows, :].astype(F32)
            outs[i][rows, :] = total.astype(outs[i].dtype)
        return 0

    lax.fori_loop(0, 4, work, 0)


def local_call(kernel, outs, name, *args, smem=True):
    vmem = pl.BlockSpec(memory_space=pltpu.VMEM)
    first = [pl.BlockSpec(memory_space=pltpu.SMEM)] if smem else []
    return pl.pallas_call(
        kernel,
        in_specs=first + [vmem] * (len(args) - len(first)),
        out_specs=[vmem] * len(outs),
        out_shape=[jax.ShapeDtypeStruct(*o) for o in outs],
        compiler_params=pltpu.CompilerParams(vmem_limit_bytes=VMEM_LIMIT),
        name=name,
    )(*args)


def attend_kernel(q, k_new, v_new, k, v, lengths, out, q_heads, o_heads):
    inv_root = HEAD_DIM ** (-0.5)
    for h in range(8):
        to = pl.ds(h, 16, stride=8)
        if h < 6:
            q_heads[to, :] = q[:, h * 128 : h * 128 + 128].astype(F32)
        else:
            q_heads[to, :] = jnp.zeros((16, 128), F32)
    queries = q_heads[...]
    own_products = queries.reshape(16, 8, 128) * k_new[...].astype(F32)[:, None, :]
    own_scores = jnp.sum(own_products, axis=2, keepdims=True) * inv_root
    narrow = queries.astype(BF16)
    scores = [
        lax.dot_general(
            narrow[r * 8 : r * 8 + 8],
            k[r],
            (((1,), (1,)), ((), ())),
            preferred_element_type=F32,
        )
        for r in range(16)
    ]
    scores = jnp.concatenate(scores, axis=0).reshape(16, 8, 192) * inv_root
    live = lax.broadcasted_iota(jnp.int32, (16, 8, 192), 2) < lengths[...].reshape(16, 1, 1)
    scores = jnp.where(live, scores, -1e30)
    peak = jnp.maximum(jnp.max(scores, axis=2, keepdims=True), own_scores)
    weights = jnp.exp(scores - peak)
    own_weights = jnp.exp(own_scores - peak)
    scale = 1.0 / (jnp.sum(weights, axis=2, keepdims=True) + own_weights)
    weights = (weights * scale).astype(BF16).reshape(128, 192)
    own_weights = (own_weights * scale).astype(BF16).astype(F32)
    own_part = own_weights * v_new[...].astype(F32)[:, None, :]
    for r in range(16):
        mixed = jnp.dot(weights[r * 8 : r * 8 + 8], v[r], preferred_element_type=F32)
        o_heads[r * 8 : r * 8 + 8, :] = mixed + own_part[r]
    for h in range(6):
        out[:, h * 128 : h * 128 + 128] = o_heads[pl.ds(h, 16, stride=8), :].astype(BF16)


def attend(q_new, k_new, v_new, k_cache, v_cache, lengths):
    def rows(*rest):
        return pl.BlockSpec((16, *rest), lambda i: (i,) + (0,) * len(rest))

    return pl.pallas_call(
        attend_kernel,
        grid=(2,),
        in_specs=[rows(768), rows(128), rows(128), rows(192, 128), rows(192, 128), rows(1)],
        out_specs=rows(768),
        out_shape=jax.ShapeDtypeStruct((32, 768), BF16),
        scratch_shapes=[pltpu.VMEM((128, 128), F32)] * 2,
        compiler_params=pltpu.CompilerParams(vmem_limit_bytes=VMEM_LIMIT),
        name="attend",
    )(q_new, k_new, v_new, k_cache, v_cache, lengths.reshape(32, 1))


def ranks_of(member):
    n = member.shape[0]
    lower = (
        lax.broadcasted_iota(jnp.int32, (n, n), 0) >= lax.broadcasted_iota(jnp.int32, (n, n), 1)
    ).astype(BF16)
    counts = jnp.dot(lower, member.astype(BF16), preferred_element_type=F32).astype(jnp.int32)
    return jnp.where(member, counts - 1, -1)


def shards(
    q_new,
    k_new,
    v_new,
    k_cache,
    v_cache,
    lengths,
    attn_out_weight,
    residual,
    norm_gain,
    router_weight,
    expert_ids,
    gate_weight,
    up_weight,
    down_weight,
):
    chip = lax.axis_index("dp")
    core = lax.axis_index("side")
    plane = lax.axis_index("tensor")
    pos = jnp.stack([chip // 4, chip % 4, core]).astype(jnp.int32)
    first_core = core == 0

    def by_core(own, other, axis):
        return jnp.where(
            first_core,
            jnp.concatenate([own, other], axis=axis),
            jnp.concatenate([other, own], axis=axis),
        )

    def half(a):
        return jnp.where(first_core, a[:, :192], a[:, 192:])

    attention = attend(q_new, k_new, v_new, k_cache, v_cache, lengths)
    residual_chip = by_core(residual, swap_cores(residual), 1).reshape(2, 2, 32, 384)
    residual_half = jnp.where(first_core, residual_chip[:, 0], residual_chip[:, 1])

    labels = jnp.arange(EXPERTS, dtype=jnp.int32)
    block_ids = lax.dynamic_slice_in_dim(expert_ids, plane * 128, 128, 0)
    member = jnp.any(block_ids[:, :, None] == labels, axis=1)
    ranks = ranks_of(member).T
    ranks_by_core = ranks.reshape(8, 2, 2, 32).transpose(0, 2, 1, 3).reshape(8, 128)
    slots = jnp.arange(32, dtype=jnp.int32)

    def pick(ranks, side):
        return (ranks[:, None, :] - side * 32 == slots[:, None]).astype(BF16).reshape(256, 128)

    pick_routed = pick(ranks_by_core, core)
    pick_own, pick_other = pick(ranks, core), pick(ranks, 1 - core)
    ids_by_block = expert_ids.reshape(8, 128, 2)
    named = jnp.any(ids_by_block == plane, axis=2)
    ranks_mine = ranks_of(named.T).T
    partner_ids = jnp.sum(ids_by_block, axis=2) - plane
    hits = ranks_mine[:, None, :] - core * 32 == slots[:, None]
    partner = jnp.sum(jnp.where(hits, partner_ids[:, None, :], 0), axis=2).reshape(256, 1)
    signs = (labels == plane).astype(F32) - (labels == partner).astype(F32)

    rows_x = [lax.ppermute(attention, "dp", SHIFT_X[d]) for d in (1, 2, 3)]
    columns, rows_x[2] = lax.optimization_barrier((attn_out_weight, rows_x[2]))
    out_w = by_core(columns, swap_cores(columns), 1)
    rows_x = jnp.stack([attention] + rows_x)
    rows_xy = [rows_x] + [lax.ppermute(rows_x, "dp", SHIFT_Y[d]) for d in (1, 2, 3)]
    vmem = pl.BlockSpec(memory_space=pltpu.VMEM)
    head_sums = pl.pallas_call(
        outproj_kernel,
        in_specs=[pl.BlockSpec(memory_space=pltpu.SMEM)] + [vmem] * 5,
        out_specs=vmem,
        out_shape=jax.ShapeDtypeStruct((8, 64, 384), BF16),
        compiler_params=pltpu.CompilerParams(vmem_limit_bytes=VMEM_LIMIT),
        name="out_projection",
    )(pos, *rows_xy, out_w)
    heads_in = lax.all_to_all(head_sums, "tensor", split_axis=0, concat_axis=0, tiled=True)
    hidden = (
        jnp.sum(heads_in.astype(F32), axis=0) + residual_half.reshape(64, 384).astype(F32)
    ).astype(BF16)
    hidden_chip = by_core(hidden, swap_cores(hidden), 0)
    hidden_rows = half(
        hidden_chip.reshape(2, 2, 32, 384).transpose(1, 0, 2, 3).reshape(128, 384)
    )
    routed = jnp.dot(pick_routed, hidden_chip, preferred_element_type=F32).astype(BF16)
    mine = lax.all_to_all(
        routed.reshape(8, 32, 384), "tensor", split_axis=0, concat_axis=0, tiled=True
    ).reshape(256, 384)

    a, b = mine[:128], mine[128:]
    got = lax.optimization_barrier(
        [lax.ppermute(a, "dp", SHIFT_X[d]) for d in (1, 2, 3)]
        + [lax.ppermute(b, "dp", SHIFT_Y[d]) for d in (1, 2, 3)]
    )
    stack_a, stack_b = jnp.stack([a] + got[:3]), jnp.stack([b] + got[3:])
    gate_w, up_w, down_w = gate_weight[0], up_weight[0], down_weight[0]
    a1, a3, b1, b3 = [lax.ppermute(stack_a, "dp", SHIFT_Y[d]) for d in (1, 3)] + [
        lax.ppermute(stack_b, "dp", SHIFT_X[d]) for d in (1, 3)
    ]
    far_a, far_b, a1, b1 = lax.optimization_barrier((stack_a, stack_b, a1, b1))
    a2, b2 = lax.ppermute(far_a, "dp", SHIFT_Y[2]), lax.ppermute(far_b, "dp", SHIFT_X[2])
    gain = norm_gain.reshape(16, 1, 384)
    normed = local_call(
        norm_kernel,
        [((256, 6144), BF16)],
        "norm",
        pos,
        *(stack_a, a1, a2, a3),
        *(stack_b, b1, b2, b3),
        gain,
    )[0]
    normed_other = swap_cores(normed)

    def expert_in(rows):
        gate = jnp.dot(rows, gate_w, preferred_element_type=F32)
        up = jnp.dot(rows, up_w, preferred_element_type=F32)
        return (jax.nn.silu(gate) * up).astype(BF16)

    def expert_out_of(rows):
        return jnp.dot(rows, down_w, preferred_element_type=F32).astype(BF16)

    logits = jnp.dot(normed, router_weight, preferred_element_type=F32)
    shares = jax.nn.sigmoid(jnp.sum(logits * signs, axis=1, keepdims=True))
    inner = expert_in(normed)
    inner, normed_other = lax.optimization_barrier((inner, normed_other))
    own = expert_out_of(inner)
    inner_other = expert_in(normed_other)
    other = [swap_cores(expert_out_of(inner_other[r : r + 128])) for r in (0, 128)]

    expert_out = []
    for h in (0, 1):
        near, far = (SHIFT_Y, SHIFT_X) if h == 0 else (SHIFT_X, SHIFT_Y)
        stack = (4, 128, 384)
        sums = local_call(
            combine_kernel(h),
            [(stack, BF16)] * 4,
            "combine_cores",
            pos,
            own,
            other[h],
        )
        got = [lax.ppermute(sums[d], "dp", near[d]) for d in (1, 3, 2)]
        rows = local_call(
            rows_kernel,
            [((128, 384), F32)] + [((128, 384), BF16)] * 3,
            "sum_rows",
            sums[0],
            *got,
            smem=False,
        )
        got = [lax.ppermute(rows[d], "dp", far[d]) for d in (1, 3, 2)]
        expert_out.append(rows[0] + sum(g.astype(F32) for g in got))
    expert_out = jnp.concatenate(expert_out)

    parts = (shares * expert_out).astype(BF16)
    back = lax.all_to_all(
        parts.reshape(8, 32, 384), "tensor", split_axis=0, concat_axis=0, tiled=True
    ).reshape(256, 384)
    keep = half(back)
    taken = swap_cores(jnp.where(first_core, back[:, 192:], back[:, :192]))

    def spread(pick, rows):
        return lax.dot_general(pick, rows, (((0,), (0,)), ((), ())), preferred_element_type=F32)

    return (hidden_rows.astype(F32) + spread(pick_own, keep) + spread(pick_other, taken)).astype(
        BF16
    )


def solution(mesh):
    return jax.shard_map(
        shards,
        mesh=mesh,
        in_specs=(
            P(("dp", "side"), "tensor"),
            P(("dp", "side"), "tensor"),
            P(("dp", "side"), "tensor"),
            P(("dp", "side"), None, "tensor"),
            P(("dp", "side"), None, "tensor"),
            P(("dp", "side")),
            P("tensor", ("dp", "side")),
            P("tensor", ("dp", "side")),
            P(),
            P(),
            P(),
            P("tensor", None, ("dp", "side")),
            P("tensor", None, ("dp", "side")),
            P("tensor", ("dp", "side"), None),
        ),
        out_specs=P("tensor", ("dp", "side")),
        check_vma=False,
    )
```

```python
import jax
import jax.numpy as jnp
from jax import lax
from jax.experimental import pallas as pl
from jax.experimental.pallas import tpu as pltpu
from jax.sharding import PartitionSpec as P

HEAD_DIM = 128
EXPERTS = 8
eps = 1e-05
F32 = jnp.float32
BF16 = jnp.bfloat16
VMEM_LIMIT = 16 * 1024 * 1024
ALL_VMEM = 60 * 1024 * 1024

SHIFT_X = [[(4 * x + y, 4 * ((x + d) % 4) + y) for x in range(4) for y in range(4)] for d in range(4)]
SHIFT_Y = [[(4 * x + y, 4 * x + (y + d) % 4) for x in range(4) for y in range(4)] for d in range(4)]
SWAP = [(0, 1), (1, 0)]


def swap_cores(a):
    return lax.ppermute(a, "side", SWAP)


def chip_at(pos, dx, dy):
    return ((pos[0] + dx) & 3) * 4 + ((pos[1] + dy) & 3)


def outproj_kernel(pos, g0, g1, g2, g3, w_own, w_other, out, w):
    core = pos[2]
    w[pl.ds(pl.multiple_of(core * 192, 64), 192), :] = w_own[...]
    w[pl.ds(pl.multiple_of((1 - core) * 192, 64), 192), :] = w_other[...]
    for dy, ref in enumerate((g0, g1, g2, g3)):
        sums = lax.dot_general(
            ref[...].reshape(128, 768),
            w[...],
            (((1,), (1,)), ((), ())),
            preferred_element_type=F32,
        ).astype(BF16)
        for dx in range(4):
            chip = chip_at(pos, -dx, -dy)
            row = pl.multiple_of((chip & 1) * 32, 32)
            out[chip // 2, pl.ds(row, 32), :] = sums[dx * 32 : dx * 32 + 32]


def at_half(pos, h, i, shift):
    return chip_at(pos, i, shift) if h == 0 else chip_at(pos, shift, i)


def norm_kernel(pos, a0, a1, a2, a3, b0, b1, b2, b3, gain, out):
    for h, refs in ((0, (a0, a1, a2, a3)), (1, (b0, b1, b2, b3))):

        def rows_of(n, _, h=h, refs=refs):
            rows = pl.ds(pl.multiple_of(n * 32, 32), 32)
            to = pl.ds(pl.multiple_of(h * 128 + n * 32, 32), 32)

            def square(j, total):
                for i in range(4):
                    v = refs[i][j, rows, :].astype(F32)
                    total = total + v * v
                return total

            squares = lax.fori_loop(0, 4, square, jnp.zeros((32, 384), F32))
            mean = jnp.sum(squares, axis=1, keepdims=True) * (1.0 / 6144.0)
            scale = lax.rsqrt(mean + eps)

            def store(j, _):
                for i in range(4):
                    chip = at_half(pos, h, -j, -i)
                    columns = pl.ds(pl.multiple_of(chip * 384, 128), 384)
                    v = refs[i][j, rows, :].astype(F32)
                    out[to, columns] = (v * scale * gain[chip]).astype(BF16)
                return 0

            lax.fori_loop(0, 4, store, 0)
            return 0

        lax.fori_loop(0, 4, rows_of, 0)


def combine_kernel(h):
    def kernel(pos, own, other, *outs):
        def work(n, _):
            i, rows = n // 4, pl.ds(pl.multiple_of((n % 4) * 32, 32), 32)
            to = pl.ds(pl.multiple_of(h * 128 + (n % 4) * 32, 32), 32)
            for k in range(4):
                columns = pl.ds(pl.multiple_of(at_half(pos, h, i, k) * 384, 128), 384)
                outs[k][i, rows, :] = own[to, columns] + other[rows, columns]
            return 0

        lax.fori_loop(0, 16, work, 0)

    return kernel


def rows_kernel(mine, got1, got2, got3, *outs):
    def work(n, _):
        rows = pl.ds(pl.multiple_of(n * 32, 32), 32)
        for i in range(4):
            total = mine[i, rows, :].astype(F32)
            for got in (got1, got2, got3):
                total = total + got[i, rows, :].astype(F32)
            outs[i][rows, :] = total.astype(outs[i].dtype)
        return 0

    lax.fori_loop(0, 4, work, 0)


def local_call(kernel, outs, name, *args, smem=True):
    vmem = pl.BlockSpec(memory_space=pltpu.VMEM)
    first = [pl.BlockSpec(memory_space=pltpu.SMEM)] if smem else []
    return pl.pallas_call(
        kernel,
        in_specs=first + [vmem] * (len(args) - len(first)),
        out_specs=[vmem] * len(outs),
        out_shape=[jax.ShapeDtypeStruct(*o) for o in outs],
        compiler_params=pltpu.CompilerParams(vmem_limit_bytes=VMEM_LIMIT),
        name=name,
    )(*args)


def attend_kernel(lengths, q_in, k_in, v_in, keys, values, out, *scratch):
    q, k_new, v_new, k, v, q_heads, o_heads, sems, block_sems = scratch
    inv_root = HEAD_DIM ** (-0.5)
    small = [
        pltpu.make_async_copy(ref, to, sems.at[n])
        for n, (ref, to) in enumerate(((q_in, q), (k_in, k_new), (v_in, v_new)))
    ]

    def block_copies(b):
        rows = pl.ds(pl.multiple_of(b * 16, 16), 16)
        return (
            pltpu.make_async_copy(keys.at[rows], k.at[rows], block_sems.at[b, 0]),
            pltpu.make_async_copy(values.at[rows], v.at[rows], block_sems.at[b, 1]),
        )

    for copy in small:
        copy.start()
    for b in range(2):
        for copy in block_copies(b):
            copy.start()
    for copy in small:
        copy.wait()

    def block(b, _):
        rows = pl.ds(pl.multiple_of(b * 16, 16), 16)
        for h in range(8):
            to = pl.ds(h, 16, stride=8)
            if h < 6:
                q_heads[to, :] = q[rows, h * 128 : h * 128 + 128].astype(F32)
            else:
                q_heads[to, :] = jnp.zeros((16, 128), F32)
        queries = q_heads[...]
        own_products = queries.reshape(16, 8, 128) * k_new[rows, :].astype(F32)[:, None, :]
        own_scores = jnp.sum(own_products, axis=2, keepdims=True) * inv_root
        narrow = queries.astype(BF16)
        position = lax.broadcasted_iota(jnp.int32, (8, 192), 1)
        key_copy, value_copy = block_copies(b)
        key_copy.wait()
        scores = []
        for r in range(16):
            products = lax.dot_general(
                narrow[r * 8 : r * 8 + 8],
                k[b * 16 + r],
                (((1,), (1,)), ((), ())),
                preferred_element_type=F32,
            )
            live = position < lengths[b * 16 + r]
            scores.append(jnp.where(live, products * inv_root, -1e30))
        scores = jnp.concatenate(scores, axis=0).reshape(16, 8, 192)
        peak = jnp.maximum(jnp.max(scores, axis=2, keepdims=True), own_scores)
        weights = jnp.exp(scores - peak)
        own_weights = jnp.exp(own_scores - peak)
        scale = 1.0 / (jnp.sum(weights, axis=2, keepdims=True) + own_weights)
        weights = (weights * scale).astype(BF16).reshape(128, 192)
        own_weights = (own_weights * scale).astype(BF16).astype(F32)
        own_part = own_weights * v_new[rows, :].astype(F32)[:, None, :]
        value_copy.wait()
        for r in range(16):
            mixed = jnp.dot(
                weights[r * 8 : r * 8 + 8], v[b * 16 + r], preferred_element_type=F32
            )
            o_heads[r * 8 : r * 8 + 8, :] = mixed + own_part[r]
        for h in range(6):
            heads = o_heads[pl.ds(h, 16, stride=8), :]
            out[rows, h * 128 : h * 128 + 128] = heads.astype(BF16)
        return 0

    lax.fori_loop(0, 2, block, 0)


def attend(q_new, k_new, v_new, k_cache, v_cache, lengths):
    hbm = pl.BlockSpec(memory_space=pltpu.HBM)
    return pl.pallas_call(
        attend_kernel,
        in_specs=[pl.BlockSpec(memory_space=pltpu.SMEM)] + [hbm] * 5,
        out_specs=pl.BlockSpec(memory_space=pltpu.VMEM),
        out_shape=jax.ShapeDtypeStruct((32, 768), BF16),
        scratch_shapes=[
            pltpu.VMEM((32, 768), BF16),
            pltpu.VMEM((32, 128), BF16),
            pltpu.VMEM((32, 128), BF16),
            pltpu.VMEM((32, 192, 128), BF16),
            pltpu.VMEM((32, 192, 128), BF16),
            pltpu.VMEM((128, 128), F32),
            pltpu.VMEM((128, 128), F32),
            pltpu.SemaphoreType.DMA((3,)),
            pltpu.SemaphoreType.DMA((2, 2)),
        ],
        compiler_params=pltpu.CompilerParams(vmem_limit_bytes=ALL_VMEM),
        name="attend",
    )(lengths, q_new, k_new, v_new, k_cache, v_cache)


def ranks_of(member):
    n = member.shape[0]
    lower = (
        lax.broadcasted_iota(jnp.int32, (n, n), 0) >= lax.broadcasted_iota(jnp.int32, (n, n), 1)
    ).astype(BF16)
    counts = jnp.dot(lower, member.astype(BF16), preferred_element_type=F32).astype(jnp.int32)
    return jnp.where(member, counts - 1, -1)


def shards(
    q_new,
    k_new,
    v_new,
    k_cache,
    v_cache,
    lengths,
    attn_out_weight,
    residual,
    norm_gain,
    router_weight,
    expert_ids,
    gate_weight,
    up_weight,
    down_weight,
):
    chip = lax.axis_index("dp")
    core = lax.axis_index("side")
    plane = lax.axis_index("tensor")
    pos = jnp.stack([chip // 4, chip % 4, core]).astype(jnp.int32)
    first_core = core == 0

    def by_core(own, other, axis):
        return jnp.where(
            first_core,
            jnp.concatenate([own, other], axis=axis),
            jnp.concatenate([other, own], axis=axis),
        )

    def half(a):
        return jnp.where(first_core, a[:, :192], a[:, 192:])

    attention = attend(q_new, k_new, v_new, k_cache, v_cache, lengths)
    residual_chip = by_core(residual, swap_cores(residual), 1).reshape(2, 2, 32, 384)
    residual_half = jnp.where(first_core, residual_chip[:, 0], residual_chip[:, 1])

    labels = jnp.arange(EXPERTS, dtype=jnp.int32)
    block_ids = lax.dynamic_slice_in_dim(expert_ids, plane * 128, 128, 0)
    member = jnp.any(block_ids[:, :, None] == labels, axis=1)
    ranks = ranks_of(member).T
    ranks_by_core = ranks.reshape(8, 2, 2, 32).transpose(0, 2, 1, 3).reshape(8, 128)
    slots = jnp.arange(32, dtype=jnp.int32)

    def pick(ranks, side):
        return (ranks[:, None, :] - side * 32 == slots[:, None]).astype(BF16).reshape(256, 128)

    pick_routed = pick(ranks_by_core, core)
    pick_own, pick_other = pick(ranks, core), pick(ranks, 1 - core)
    ids_by_block = expert_ids.reshape(8, 128, 2)
    named = jnp.any(ids_by_block == plane, axis=2)
    ranks_mine = ranks_of(named.T).T
    partner_ids = jnp.sum(ids_by_block, axis=2) - plane
    hits = ranks_mine[:, None, :] - core * 32 == slots[:, None]
    partner = jnp.sum(jnp.where(hits, partner_ids[:, None, :], 0), axis=2).reshape(256, 1)
    signs = (labels == plane).astype(F32) - (labels == partner).astype(F32)

    rows_x = [lax.ppermute(attention, "dp", SHIFT_X[d]) for d in (1, 2, 3)]
    out_w = attn_out_weight.T
    out_w_other = swap_cores(out_w)
    rows_x = jnp.stack([attention] + rows_x)
    rows_xy = [rows_x] + [lax.ppermute(rows_x, "dp", SHIFT_Y[d]) for d in (1, 2, 3)]
    vmem = pl.BlockSpec(memory_space=pltpu.VMEM)
    head_sums = pl.pallas_call(
        outproj_kernel,
        in_specs=[pl.BlockSpec(memory_space=pltpu.SMEM)] + [vmem] * 6,
        out_specs=vmem,
        out_shape=jax.ShapeDtypeStruct((8, 64, 384), BF16),
        scratch_shapes=[pltpu.VMEM((384, 768), BF16)],
        compiler_params=pltpu.CompilerParams(vmem_limit_bytes=VMEM_LIMIT),
        name="out_projection",
    )(pos, *rows_xy, out_w, out_w_other)
    heads_in = lax.all_to_all(head_sums, "tensor", split_axis=0, concat_axis=0, tiled=True)
    hidden = (
        jnp.sum(heads_in.astype(F32), axis=0) + residual_half.reshape(64, 384).astype(F32)
    ).astype(BF16)
    hidden_chip = by_core(hidden, swap_cores(hidden), 0)
    hidden_rows = half(
        hidden_chip.reshape(2, 2, 32, 384).transpose(1, 0, 2, 3).reshape(128, 384)
    )
    routed = jnp.dot(pick_routed, hidden_chip, preferred_element_type=F32).astype(BF16)
    mine = lax.all_to_all(
        routed.reshape(8, 32, 384), "tensor", split_axis=0, concat_axis=0, tiled=True
    ).reshape(256, 384)

    a, b = mine[:128], mine[128:]
    got = lax.optimization_barrier(
        [lax.ppermute(a, "dp", SHIFT_X[d]) for d in (1, 2, 3)]
        + [lax.ppermute(b, "dp", SHIFT_Y[d]) for d in (1, 2, 3)]
    )
    stack_a, stack_b = jnp.stack([a] + got[:3]), jnp.stack([b] + got[3:])
    gate_w, up_w, down_w = gate_weight[0], up_weight[0], down_weight[0]
    a1, a3, b1, b3 = [lax.ppermute(stack_a, "dp", SHIFT_Y[d]) for d in (1, 3)] + [
        lax.ppermute(stack_b, "dp", SHIFT_X[d]) for d in (1, 3)
    ]
    far_a, far_b, a1, b1 = lax.optimization_barrier((stack_a, stack_b, a1, b1))
    a2, b2 = lax.ppermute(far_a, "dp", SHIFT_Y[2]), lax.ppermute(far_b, "dp", SHIFT_X[2])
    gain = norm_gain.reshape(16, 1, 384)
    normed = local_call(
        norm_kernel,
        [((256, 6144), BF16)],
        "norm",
        pos,
        *(stack_a, a1, a2, a3),
        *(stack_b, b1, b2, b3),
        gain,
    )[0]
    normed_other = swap_cores(normed)

    def expert_in(rows):
        gate = jnp.dot(rows, gate_w, preferred_element_type=F32)
        up = jnp.dot(rows, up_w, preferred_element_type=F32)
        return (jax.nn.silu(gate) * up).astype(BF16)

    def expert_out_of(rows):
        return jnp.dot(rows, down_w, preferred_element_type=F32).astype(BF16)

    logits = jnp.dot(normed, router_weight, preferred_element_type=F32)
    shares = jax.nn.sigmoid(jnp.sum(logits * signs, axis=1, keepdims=True))
    inner = expert_in(normed)
    own = expert_out_of(inner)
    own, normed_other = lax.optimization_barrier((own, normed_other))
    inner_other = expert_in(normed_other)
    other = [swap_cores(expert_out_of(inner_other[r : r + 128])) for r in (0, 128)]

    expert_out = []
    for h in (0, 1):
        near, far = (SHIFT_Y, SHIFT_X) if h == 0 else (SHIFT_X, SHIFT_Y)
        stack = (4, 128, 384)
        sums = local_call(
            combine_kernel(h),
            [(stack, BF16)] * 4,
            "combine_cores",
            pos,
            own,
            other[h],
        )
        got = [lax.ppermute(sums[d], "dp", near[d]) for d in (1, 3, 2)]
        rows = local_call(
            rows_kernel,
            [((128, 384), F32)] + [((128, 384), BF16)] * 3,
            "sum_rows",
            sums[0],
            *got,
            smem=False,
        )
        got = [lax.ppermute(rows[d], "dp", far[d]) for d in (1, 3, 2)]
        expert_out.append(rows[0] + sum(g.astype(F32) for g in got))
    expert_out = jnp.concatenate(expert_out)

    parts = (shares * expert_out).astype(BF16)
    back = lax.all_to_all(
        parts.reshape(8, 32, 384), "tensor", split_axis=0, concat_axis=0, tiled=True
    ).reshape(256, 384)
    keep = half(back)
    taken = swap_cores(jnp.where(first_core, back[:, 192:], back[:, :192]))

    def spread(pick, rows):
        return lax.dot_general(pick, rows, (((0,), (0,)), ((), ())), preferred_element_type=F32)

    return (hidden_rows.astype(F32) + spread(pick_own, keep) + spread(pick_other, taken)).astype(
        BF16
    )


def solution(mesh):
    return jax.shard_map(
        shards,
        mesh=mesh,
        in_specs=(
            P(("dp", "side"), "tensor"),
            P(("dp", "side"), "tensor"),
            P(("dp", "side"), "tensor"),
            P(("dp", "side"), None, "tensor"),
            P(("dp", "side"), None, "tensor"),
            P(("dp", "side")),
            P("tensor", ("dp", "side")),
            P("tensor", ("dp", "side")),
            P(),
            P(),
            P(),
            P("tensor", None, ("dp", "side")),
            P("tensor", None, ("dp", "side")),
            P("tensor", ("dp", "side"), None),
        ),
        out_specs=P("tensor", ("dp", "side")),
        check_vma=False,
    )
```

```python
import jax
import jax.numpy as jnp
from jax import lax
from jax.experimental import pallas as pl
from jax.experimental.pallas import tpu as pltpu
from jax.sharding import PartitionSpec as P

HEAD_DIM = 128
EXPERTS = 8
eps = 1e-05
F32 = jnp.float32
BF16 = jnp.bfloat16
VMEM_LIMIT = 16 * 1024 * 1024
ALL_VMEM = 60 * 1024 * 1024

SHIFT_X = [[(4 * x + y, 4 * ((x + d) % 4) + y) for x in range(4) for y in range(4)] for d in range(4)]
SHIFT_Y = [[(4 * x + y, 4 * x + (y + d) % 4) for x in range(4) for y in range(4)] for d in range(4)]
SWAP = [(0, 1), (1, 0)]


def swap_cores(a):
    return lax.ppermute(a, "side", SWAP)


def chip_at(pos, dx, dy):
    return ((pos[0] + dx) & 3) * 4 + ((pos[1] + dy) & 3)


def outproj_kernel(pos, g0, g1, g2, g3, w_own, w_other, out, w):
    core = pos[2]
    w[pl.ds(pl.multiple_of(core * 192, 64), 192), :] = w_own[...]
    w[pl.ds(pl.multiple_of((1 - core) * 192, 64), 192), :] = w_other[...]
    for dy, ref in enumerate((g0, g1, g2, g3)):
        sums = lax.dot_general(
            ref[...].reshape(128, 768),
            w[...],
            (((1,), (1,)), ((), ())),
            preferred_element_type=F32,
        ).astype(BF16)
        for dx in range(4):
            chip = chip_at(pos, -dx, -dy)
            row = pl.multiple_of((chip & 1) * 32, 32)
            out[chip // 2, pl.ds(row, 32), :] = sums[dx * 32 : dx * 32 + 32]


def at_half(pos, h, i, shift):
    return chip_at(pos, i, shift) if h == 0 else chip_at(pos, shift, i)


def norm_kernel(pos, a0, a1, a2, a3, b0, b1, b2, b3, gain, out):
    for h, refs in ((0, (a0, a1, a2, a3)), (1, (b0, b1, b2, b3))):

        def rows_of(n, _, h=h, refs=refs):
            rows = pl.ds(pl.multiple_of(n * 32, 32), 32)
            to = pl.ds(pl.multiple_of(h * 128 + n * 32, 32), 32)

            def square(j, total):
                for i in range(4):
                    v = refs[i][j, rows, :].astype(F32)
                    total = total + v * v
                return total

            squares = lax.fori_loop(0, 4, square, jnp.zeros((32, 384), F32))
            mean = jnp.sum(squares, axis=1, keepdims=True) * (1.0 / 6144.0)
            scale = lax.rsqrt(mean + eps)

            def store(j, _):
                for i in range(4):
                    chip = at_half(pos, h, -j, -i)
                    columns = pl.ds(pl.multiple_of(chip * 384, 128), 384)
                    v = refs[i][j, rows, :].astype(F32)
                    out[to, columns] = (v * scale * gain[chip]).astype(BF16)
                return 0

            lax.fori_loop(0, 4, store, 0)
            return 0

        lax.fori_loop(0, 4, rows_of, 0)


def combine_kernel(h):
    def kernel(pos, own, other, *outs):
        def work(n, _):
            i, rows = n // 4, pl.ds(pl.multiple_of((n % 4) * 32, 32), 32)
            to = pl.ds(pl.multiple_of(h * 128 + (n % 4) * 32, 32), 32)
            for k in range(4):
                columns = pl.ds(pl.multiple_of(at_half(pos, h, i, k) * 384, 128), 384)
                outs[k][i, rows, :] = own[to, columns] + other[rows, columns]
            return 0

        lax.fori_loop(0, 16, work, 0)

    return kernel


def rows_kernel(mine, got1, got2, got3, *outs):
    def work(n, _):
        rows = pl.ds(pl.multiple_of(n * 32, 32), 32)
        for i in range(4):
            total = mine[i, rows, :].astype(F32)
            for got in (got1, got2, got3):
                total = total + got[i, rows, :].astype(F32)
            outs[i][rows, :] = total.astype(outs[i].dtype)
        return 0

    lax.fori_loop(0, 4, work, 0)


def local_call(kernel, outs, name, *args, smem=True):
    vmem = pl.BlockSpec(memory_space=pltpu.VMEM)
    first = [pl.BlockSpec(memory_space=pltpu.SMEM)] if smem else []
    return pl.pallas_call(
        kernel,
        in_specs=first + [vmem] * (len(args) - len(first)),
        out_specs=[vmem] * len(outs),
        out_shape=[jax.ShapeDtypeStruct(*o) for o in outs],
        compiler_params=pltpu.CompilerParams(vmem_limit_bytes=VMEM_LIMIT),
        name=name,
    )(*args)


def attend_kernel(lengths, q_in, k_in, v_in, keys, values, out, *scratch):
    q, k_new, v_new, k, v, q_heads, o_heads, sems, block_sems = scratch
    inv_root = HEAD_DIM ** (-0.5)
    small = [
        pltpu.make_async_copy(ref, to, sems.at[n])
        for n, (ref, to) in enumerate(((q_in, q), (k_in, k_new), (v_in, v_new)))
    ]

    def block_copies(b):
        rows = pl.ds(pl.multiple_of(b * 16, 16), 16)
        return (
            pltpu.make_async_copy(keys.at[rows], k.at[rows], block_sems.at[b, 0]),
            pltpu.make_async_copy(values.at[rows], v.at[rows], block_sems.at[b, 1]),
        )

    for copy in small:
        copy.start()
    for b in range(2):
        for copy in block_copies(b):
            copy.start()
    for copy in small:
        copy.wait()

    def block(b, _):
        rows = pl.ds(pl.multiple_of(b * 16, 16), 16)
        for h in range(8):
            to = pl.ds(h, 16, stride=8)
            if h < 6:
                q_heads[to, :] = q[rows, h * 128 : h * 128 + 128].astype(F32)
            else:
                q_heads[to, :] = jnp.zeros((16, 128), F32)
        queries = q_heads[...]
        own_products = queries.reshape(16, 8, 128) * k_new[rows, :].astype(F32)[:, None, :]
        own_scores = jnp.sum(own_products, axis=2, keepdims=True) * inv_root
        narrow = queries.astype(BF16)
        position = lax.broadcasted_iota(jnp.int32, (8, 192), 1)
        key_copy, value_copy = block_copies(b)
        key_copy.wait()
        scores = []
        for r in range(16):
            products = lax.dot_general(
                narrow[r * 8 : r * 8 + 8],
                k[b * 16 + r],
                (((1,), (1,)), ((), ())),
                preferred_element_type=F32,
            )
            live = position < lengths[b * 16 + r]
            scores.append(jnp.where(live, products * inv_root, -1e30))
        scores = jnp.concatenate(scores, axis=0).reshape(16, 8, 192)
        peak = jnp.maximum(jnp.max(scores, axis=2, keepdims=True), own_scores)
        weights = jnp.exp(scores - peak)
        own_weights = jnp.exp(own_scores - peak)
        scale = 1.0 / (jnp.sum(weights, axis=2, keepdims=True) + own_weights)
        weights = (weights * scale).astype(BF16).reshape(128, 192)
        own_weights = (own_weights * scale).astype(BF16).astype(F32)
        own_part = own_weights * v_new[rows, :].astype(F32)[:, None, :]
        value_copy.wait()
        for r in range(16):
            mixed = jnp.dot(
                weights[r * 8 : r * 8 + 8], v[b * 16 + r], preferred_element_type=F32
            )
            o_heads[r * 8 : r * 8 + 8, :] = mixed + own_part[r]
        for h in range(6):
            heads = o_heads[pl.ds(h, 16, stride=8), :]
            out[rows, h * 128 : h * 128 + 128] = heads.astype(BF16)
        return 0

    lax.fori_loop(0, 2, block, 0)


def attend(q_new, k_new, v_new, k_cache, v_cache, lengths):
    hbm = pl.BlockSpec(memory_space=pltpu.HBM)
    return pl.pallas_call(
        attend_kernel,
        in_specs=[pl.BlockSpec(memory_space=pltpu.SMEM)] + [hbm] * 5,
        out_specs=pl.BlockSpec(memory_space=pltpu.VMEM),
        out_shape=jax.ShapeDtypeStruct((32, 768), BF16),
        scratch_shapes=[
            pltpu.VMEM((32, 768), BF16),
            pltpu.VMEM((32, 128), BF16),
            pltpu.VMEM((32, 128), BF16),
            pltpu.VMEM((32, 192, 128), BF16),
            pltpu.VMEM((32, 192, 128), BF16),
            pltpu.VMEM((128, 128), F32),
            pltpu.VMEM((128, 128), F32),
            pltpu.SemaphoreType.DMA((3,)),
            pltpu.SemaphoreType.DMA((2, 2)),
        ],
        compiler_params=pltpu.CompilerParams(vmem_limit_bytes=ALL_VMEM),
        name="attend",
    )(lengths, q_new, k_new, v_new, k_cache, v_cache)


def ranks_of(member):
    n = member.shape[0]
    lower = (
        lax.broadcasted_iota(jnp.int32, (n, n), 0) >= lax.broadcasted_iota(jnp.int32, (n, n), 1)
    ).astype(BF16)
    counts = jnp.dot(lower, member.astype(BF16), preferred_element_type=F32).astype(jnp.int32)
    return jnp.where(member, counts - 1, -1)


def shards(
    q_new,
    k_new,
    v_new,
    k_cache,
    v_cache,
    lengths,
    attn_out_weight,
    residual,
    norm_gain,
    router_weight,
    expert_ids,
    gate_weight,
    up_weight,
    down_weight,
):
    chip = lax.axis_index("dp")
    core = lax.axis_index("side")
    plane = lax.axis_index("tensor")
    pos = jnp.stack([chip // 4, chip % 4, core]).astype(jnp.int32)
    first_core = core == 0

    def by_core(own, other, axis):
        return jnp.where(
            first_core,
            jnp.concatenate([own, other], axis=axis),
            jnp.concatenate([other, own], axis=axis),
        )

    def half(a):
        return jnp.where(first_core, a[:, :192], a[:, 192:])

    attention = attend(q_new, k_new, v_new, k_cache, v_cache, lengths)
    residual_chip = by_core(residual, swap_cores(residual), 1).reshape(2, 2, 32, 384)
    residual_half = jnp.where(first_core, residual_chip[:, 0], residual_chip[:, 1])

    labels = jnp.arange(EXPERTS, dtype=jnp.int32)
    block_ids = lax.dynamic_slice_in_dim(expert_ids, plane * 128, 128, 0)
    member = jnp.any(block_ids[:, :, None] == labels, axis=1)
    ranks = ranks_of(member).T
    ranks_by_core = ranks.reshape(8, 2, 2, 32).transpose(0, 2, 1, 3).reshape(8, 128)
    slots = jnp.arange(32, dtype=jnp.int32)

    def pick(ranks, side):
        return (ranks[:, None, :] - side * 32 == slots[:, None]).astype(BF16).reshape(256, 128)

    pick_routed = pick(ranks_by_core, core)
    pick_own, pick_other = pick(ranks, core), pick(ranks, 1 - core)
    ids_by_block = expert_ids.reshape(8, 128, 2)
    named = jnp.any(ids_by_block == plane, axis=2)
    ranks_mine = ranks_of(named.T).T
    partner_ids = jnp.sum(ids_by_block, axis=2) - plane
    hits = ranks_mine[:, None, :] - core * 32 == slots[:, None]
    partner = jnp.sum(jnp.where(hits, partner_ids[:, None, :], 0), axis=2).reshape(256, 1)
    signs = (labels == plane).astype(F32) - (labels == partner).astype(F32)

    rows_x = [lax.ppermute(attention, "dp", SHIFT_X[d]) for d in (1, 2, 3)]
    out_w = attn_out_weight.T
    out_w_other = swap_cores(out_w)
    rows_x = jnp.stack([attention] + rows_x)
    rows_xy = [rows_x] + [lax.ppermute(rows_x, "dp", SHIFT_Y[d]) for d in (1, 2, 3)]
    vmem = pl.BlockSpec(memory_space=pltpu.VMEM)
    head_sums = pl.pallas_call(
        outproj_kernel,
        in_specs=[pl.BlockSpec(memory_space=pltpu.SMEM)] + [vmem] * 6,
        out_specs=vmem,
        out_shape=jax.ShapeDtypeStruct((8, 64, 384), BF16),
        scratch_shapes=[pltpu.VMEM((384, 768), BF16)],
        compiler_params=pltpu.CompilerParams(vmem_limit_bytes=VMEM_LIMIT),
        name="out_projection",
    )(pos, *rows_xy, out_w, out_w_other)
    heads_in = lax.all_to_all(head_sums, "tensor", split_axis=0, concat_axis=0, tiled=True)
    hidden = (
        jnp.sum(heads_in.astype(F32), axis=0) + residual_half.reshape(64, 384).astype(F32)
    ).astype(BF16)
    hidden_chip = by_core(hidden, swap_cores(hidden), 0)
    hidden_rows = half(
        hidden_chip.reshape(2, 2, 32, 384).transpose(1, 0, 2, 3).reshape(128, 384)
    )
    routed = jnp.dot(pick_routed, hidden_chip, preferred_element_type=F32).astype(BF16)
    mine = lax.all_to_all(
        routed.reshape(8, 32, 384), "tensor", split_axis=0, concat_axis=0, tiled=True
    ).reshape(256, 384)

    a, b = mine[:128], mine[128:]
    got = lax.optimization_barrier(
        [lax.ppermute(a, "dp", SHIFT_X[d]) for d in (1, 2, 3)]
        + [lax.ppermute(b, "dp", SHIFT_Y[d]) for d in (1, 2, 3)]
    )
    stack_a, stack_b = jnp.stack([a] + got[:3]), jnp.stack([b] + got[3:])
    gate_w, up_w, down_w = gate_weight[0], up_weight[0], down_weight[0]
    a1, a3, b1, b3 = [lax.ppermute(stack_a, "dp", SHIFT_Y[d]) for d in (1, 3)] + [
        lax.ppermute(stack_b, "dp", SHIFT_X[d]) for d in (1, 3)
    ]
    far_a, far_b, a1, b1 = lax.optimization_barrier((stack_a, stack_b, a1, b1))
    a2, b2 = lax.ppermute(far_a, "dp", SHIFT_Y[2]), lax.ppermute(far_b, "dp", SHIFT_X[2])
    gain = norm_gain.reshape(16, 1, 384)
    normed = local_call(
        norm_kernel,
        [((256, 6144), BF16)],
        "norm",
        pos,
        *(stack_a, a1, a2, a3),
        *(stack_b, b1, b2, b3),
        gain,
    )[0]
    normed_other = swap_cores(normed)

    def expert_in(rows):
        gate = jnp.dot(rows, gate_w, preferred_element_type=F32)
        up = jnp.dot(rows, up_w, preferred_element_type=F32)
        return (jax.nn.silu(gate) * up).astype(BF16)

    def expert_out_of(rows):
        return jnp.dot(rows, down_w, preferred_element_type=F32).astype(BF16)

    logits = jnp.dot(normed, router_weight, preferred_element_type=F32)
    shares = jax.nn.sigmoid(jnp.sum(logits * signs, axis=1, keepdims=True))
    inner = expert_in(normed)
    inner, normed_other = lax.optimization_barrier((inner, normed_other))
    own = expert_out_of(inner)
    inner_other = expert_in(normed_other)
    other = [swap_cores(expert_out_of(inner_other[r : r + 128])) for r in (0, 128)]

    expert_out = []
    for h in (0, 1):
        near, far = (SHIFT_Y, SHIFT_X) if h == 0 else (SHIFT_X, SHIFT_Y)
        stack = (4, 128, 384)
        sums = local_call(
            combine_kernel(h),
            [(stack, BF16)] * 4,
            "combine_cores",
            pos,
            own,
            other[h],
        )
        got = [lax.ppermute(sums[d], "dp", near[d]) for d in (1, 3, 2)]
        rows = local_call(
            rows_kernel,
            [((128, 384), F32)] + [((128, 384), BF16)] * 3,
            "sum_rows",
            sums[0],
            *got,
            smem=False,
        )
        got = [lax.ppermute(rows[d], "dp", far[d]) for d in (1, 3, 2)]
        expert_out.append(rows[0] + sum(g.astype(F32) for g in got))
    expert_out = jnp.concatenate(expert_out)

    parts = (shares * expert_out).astype(BF16)
    back = lax.all_to_all(
        parts.reshape(8, 32, 384), "tensor", split_axis=0, concat_axis=0, tiled=True
    ).reshape(256, 384)
    keep = half(back)
    taken = swap_cores(jnp.where(first_core, back[:, 192:], back[:, :192]))

    def spread(pick, rows):
        return lax.dot_general(pick, rows, (((0,), (0,)), ((), ())), preferred_element_type=F32)

    return (hidden_rows.astype(F32) + spread(pick_own, keep) + spread(pick_other, taken)).astype(
        BF16
    )


def solution(mesh):
    return jax.shard_map(
        shards,
        mesh=mesh,
        in_specs=(
            P(("dp", "side"), "tensor"),
            P(("dp", "side"), "tensor"),
            P(("dp", "side"), "tensor"),
            P(("dp", "side"), None, "tensor"),
            P(("dp", "side"), None, "tensor"),
            P(("dp", "side")),
            P("tensor", ("dp", "side")),
            P("tensor", ("dp", "side")),
            P(),
            P(),
            P(),
            P("tensor", None, ("dp", "side")),
            P("tensor", None, ("dp", "side")),
            P("tensor", ("dp", "side"), None),
        ),
        out_specs=P("tensor", ("dp", "side")),
        check_vma=False,
    )
```

```python
import jax
import jax.numpy as jnp
from jax import lax
from jax.experimental import pallas as pl
from jax.experimental.pallas import tpu as pltpu
from jax.sharding import PartitionSpec as P

HEAD_DIM = 128
EXPERTS = 8
eps = 1e-05
F32 = jnp.float32
BF16 = jnp.bfloat16
VMEM_LIMIT = 16 * 1024 * 1024
ALL_VMEM = 60 * 1024 * 1024

SHIFT_X = [[(4 * x + y, 4 * ((x + d) % 4) + y) for x in range(4) for y in range(4)] for d in range(4)]
SHIFT_Y = [[(4 * x + y, 4 * x + (y + d) % 4) for x in range(4) for y in range(4)] for d in range(4)]
SWAP = [(0, 1), (1, 0)]


def swap_cores(a):
    return lax.ppermute(a, "side", SWAP)


def chip_at(pos, dx, dy):
    return ((pos[0] + dx) & 3) * 4 + ((pos[1] + dy) & 3)


def outproj_kernel(pos, g0, g1, g2, g3, w_own, w_other, out, w):
    core = pos[2]
    w[pl.ds(pl.multiple_of(core * 192, 64), 192), :] = w_own[...]
    w[pl.ds(pl.multiple_of((1 - core) * 192, 64), 192), :] = w_other[...]
    for dy, ref in enumerate((g0, g1, g2, g3)):
        sums = lax.dot_general(
            ref[...].reshape(128, 768),
            w[...],
            (((1,), (1,)), ((), ())),
            preferred_element_type=F32,
        ).astype(BF16)
        for dx in range(4):
            chip = chip_at(pos, -dx, -dy)
            row = pl.multiple_of((chip & 1) * 32, 32)
            out[chip // 2, pl.ds(row, 32), :] = sums[dx * 32 : dx * 32 + 32]


def at_half(pos, h, i, shift):
    return chip_at(pos, i, shift) if h == 0 else chip_at(pos, shift, i)


def norm_kernel(h):
    def kernel(pos, s0, s1, s2, s3, gain, out):
        refs = (s0, s1, s2, s3)

        def rows_of(n, _):
            rows = pl.ds(pl.multiple_of(n * 32, 32), 32)

            def square(j, total):
                for i in range(4):
                    v = refs[i][j, rows, :].astype(F32)
                    total = total + v * v
                return total

            squares = lax.fori_loop(0, 4, square, jnp.zeros((32, 384), F32))
            mean = jnp.sum(squares, axis=1, keepdims=True) * (1.0 / 6144.0)
            scale = lax.rsqrt(mean + eps)

            def store(j, _):
                for i in range(4):
                    chip = at_half(pos, h, -j, -i)
                    columns = pl.ds(pl.multiple_of(chip * 384, 128), 384)
                    v = refs[i][j, rows, :].astype(F32)
                    out[rows, columns] = (v * scale * gain[chip]).astype(BF16)
                return 0

            lax.fori_loop(0, 4, store, 0)
            return 0

        lax.fori_loop(0, 4, rows_of, 0)

    return kernel


def combine_kernel(h):
    def kernel(pos, own, other, *outs):
        def work(i, _):
            for k in range(4):
                columns = pl.ds(pl.multiple_of(at_half(pos, h, i, k) * 384, 128), 384)
                outs[k][i] = own[h * 128 : h * 128 + 128, columns] + other[:, columns]
            return 0

        lax.fori_loop(0, 4, work, 0)

    return kernel


def rows_kernel(mine, got1, got2, got3, *outs):
    def work(n, _):
        rows = pl.ds(pl.multiple_of(n * 32, 32), 32)
        for i in range(4):
            total = mine[i, rows, :].astype(F32)
            for got in (got1, got2, got3):
                total = total + got[i, rows, :].astype(F32)
            outs[i][rows, :] = total.astype(outs[i].dtype)
        return 0

    lax.fori_loop(0, 4, work, 0)


def local_call(kernel, outs, name, *args, smem=True):
    vmem = pl.BlockSpec(memory_space=pltpu.VMEM)
    first = [pl.BlockSpec(memory_space=pltpu.SMEM)] if smem else []
    return pl.pallas_call(
        kernel,
        in_specs=first + [vmem] * (len(args) - len(first)),
        out_specs=[vmem] * len(outs),
        out_shape=[jax.ShapeDtypeStruct(*o) for o in outs],
        compiler_params=pltpu.CompilerParams(vmem_limit_bytes=VMEM_LIMIT),
        name=name,
    )(*args)


def attend_kernel(lengths, q_in, k_in, v_in, keys, values, out, *scratch):
    q, k_new, v_new, k, v, q_heads, o_heads, sems, block_sems = scratch
    inv_root = HEAD_DIM ** (-0.5)
    small = [
        pltpu.make_async_copy(ref, to, sems.at[n])
        for n, (ref, to) in enumerate(((q_in, q), (k_in, k_new), (v_in, v_new)))
    ]

    def block_copies(b):
        rows = pl.ds(pl.multiple_of(b * 16, 16), 16)
        return (
            pltpu.make_async_copy(keys.at[rows], k.at[rows], block_sems.at[b, 0]),
            pltpu.make_async_copy(values.at[rows], v.at[rows], block_sems.at[b, 1]),
        )

    for copy in small:
        copy.start()
    for b in range(2):
        for copy in block_copies(b):
            copy.start()
    for copy in small:
        copy.wait()

    def block(b, _):
        rows = pl.ds(pl.multiple_of(b * 16, 16), 16)
        for h in range(8):
            to = pl.ds(h, 16, stride=8)
            if h < 6:
                q_heads[to, :] = q[rows, h * 128 : h * 128 + 128].astype(F32)
            else:
                q_heads[to, :] = jnp.zeros((16, 128), F32)
        queries = q_heads[...]
        own_products = queries.reshape(16, 8, 128) * k_new[rows, :].astype(F32)[:, None, :]
        own_scores = jnp.sum(own_products, axis=2, keepdims=True) * inv_root
        narrow = queries.astype(BF16)
        position = lax.broadcasted_iota(jnp.int32, (8, 192), 1)
        key_copy, value_copy = block_copies(b)
        key_copy.wait()
        scores = []
        for r in range(16):
            products = lax.dot_general(
                narrow[r * 8 : r * 8 + 8],
                k[b * 16 + r],
                (((1,), (1,)), ((), ())),
                preferred_element_type=F32,
            )
            live = position < lengths[b * 16 + r]
            scores.append(jnp.where(live, products * inv_root, -1e30))
        scores = jnp.concatenate(scores, axis=0).reshape(16, 8, 192)
        peak = jnp.maximum(jnp.max(scores, axis=2, keepdims=True), own_scores)
        weights = jnp.exp(scores - peak)
        own_weights = jnp.exp(own_scores - peak)
        scale = 1.0 / (jnp.sum(weights, axis=2, keepdims=True) + own_weights)
        weights = (weights * scale).astype(BF16).reshape(128, 192)
        own_weights = (own_weights * scale).astype(BF16).astype(F32)
        own_part = own_weights * v_new[rows, :].astype(F32)[:, None, :]
        value_copy.wait()
        for r in range(16):
            mixed = jnp.dot(
                weights[r * 8 : r * 8 + 8], v[b * 16 + r], preferred_element_type=F32
            )
            o_heads[r * 8 : r * 8 + 8, :] = mixed + own_part[r]
        for h in range(6):
            heads = o_heads[pl.ds(h, 16, stride=8), :]
            out[rows, h * 128 : h * 128 + 128] = heads.astype(BF16)
        return 0

    lax.fori_loop(0, 2, block, 0)


def attend(q_new, k_new, v_new, k_cache, v_cache, lengths):
    hbm = pl.BlockSpec(memory_space=pltpu.HBM)
    return pl.pallas_call(
        attend_kernel,
        in_specs=[pl.BlockSpec(memory_space=pltpu.SMEM)] + [hbm] * 5,
        out_specs=pl.BlockSpec(memory_space=pltpu.VMEM),
        out_shape=jax.ShapeDtypeStruct((32, 768), BF16),
        scratch_shapes=[
            pltpu.VMEM((32, 768), BF16),
            pltpu.VMEM((32, 128), BF16),
            pltpu.VMEM((32, 128), BF16),
            pltpu.VMEM((32, 192, 128), BF16),
            pltpu.VMEM((32, 192, 128), BF16),
            pltpu.VMEM((128, 128), F32),
            pltpu.VMEM((128, 128), F32),
            pltpu.SemaphoreType.DMA((3,)),
            pltpu.SemaphoreType.DMA((2, 2)),
        ],
        compiler_params=pltpu.CompilerParams(vmem_limit_bytes=ALL_VMEM),
        name="attend",
    )(lengths, q_new, k_new, v_new, k_cache, v_cache)


def ranks_of(member):
    n = member.shape[0]
    lower = (
        lax.broadcasted_iota(jnp.int32, (n, n), 0) >= lax.broadcasted_iota(jnp.int32, (n, n), 1)
    ).astype(BF16)
    counts = jnp.dot(lower, member.astype(BF16), preferred_element_type=F32).astype(jnp.int32)
    return jnp.where(member, counts - 1, -1)


def shards(
    q_new,
    k_new,
    v_new,
    k_cache,
    v_cache,
    lengths,
    attn_out_weight,
    residual,
    norm_gain,
    router_weight,
    expert_ids,
    gate_weight,
    up_weight,
    down_weight,
):
    chip = lax.axis_index("dp")
    core = lax.axis_index("side")
    plane = lax.axis_index("tensor")
    pos = jnp.stack([chip // 4, chip % 4, core]).astype(jnp.int32)
    first_core = core == 0

    def by_core(own, other, axis):
        return jnp.where(
            first_core,
            jnp.concatenate([own, other], axis=axis),
            jnp.concatenate([other, own], axis=axis),
        )

    def half(a):
        return jnp.where(first_core, a[:, :192], a[:, 192:])

    attention = attend(q_new, k_new, v_new, k_cache, v_cache, lengths)
    residual_chip = by_core(residual, swap_cores(residual), 1).reshape(2, 2, 32, 384)
    residual_half = jnp.where(first_core, residual_chip[:, 0], residual_chip[:, 1])

    labels = jnp.arange(EXPERTS, dtype=jnp.int32)
    block_ids = lax.dynamic_slice_in_dim(expert_ids, plane * 128, 128, 0)
    member = jnp.any(block_ids[:, :, None] == labels, axis=1)
    ranks = ranks_of(member).T
    ranks_by_core = ranks.reshape(8, 2, 2, 32).transpose(0, 2, 1, 3).reshape(8, 128)
    slots = jnp.arange(32, dtype=jnp.int32)

    def pick(ranks, side):
        return (ranks[:, None, :] - side * 32 == slots[:, None]).astype(BF16).reshape(256, 128)

    pick_routed = pick(ranks_by_core, core)
    pick_own, pick_other = pick(ranks, core), pick(ranks, 1 - core)
    ids_by_block = expert_ids.reshape(8, 128, 2)
    named = jnp.any(ids_by_block == plane, axis=2)
    ranks_mine = ranks_of(named.T).T
    partner_ids = jnp.sum(ids_by_block, axis=2) - plane
    hits = ranks_mine[:, None, :] - core * 32 == slots[:, None]
    partner = jnp.sum(jnp.where(hits, partner_ids[:, None, :], 0), axis=2).reshape(256, 1)
    signs = (labels == plane).astype(F32) - (labels == partner).astype(F32)

    rows_x = [lax.ppermute(attention, "dp", SHIFT_X[d]) for d in (1, 2, 3)]
    out_w = attn_out_weight.T
    out_w_other = swap_cores(out_w)
    rows_x = jnp.stack([attention] + rows_x)
    rows_xy = [rows_x] + [lax.ppermute(rows_x, "dp", SHIFT_Y[d]) for d in (1, 2, 3)]
    vmem = pl.BlockSpec(memory_space=pltpu.VMEM)
    head_sums = pl.pallas_call(
        outproj_kernel,
        in_specs=[pl.BlockSpec(memory_space=pltpu.SMEM)] + [vmem] * 6,
        out_specs=vmem,
        out_shape=jax.ShapeDtypeStruct((8, 64, 384), BF16),
        scratch_shapes=[pltpu.VMEM((384, 768), BF16)],
        compiler_params=pltpu.CompilerParams(vmem_limit_bytes=VMEM_LIMIT),
        name="out_projection",
    )(pos, *rows_xy, out_w, out_w_other)
    heads_in = lax.all_to_all(head_sums, "tensor", split_axis=0, concat_axis=0, tiled=True)
    hidden = (
        jnp.sum(heads_in.astype(F32), axis=0) + residual_half.reshape(64, 384).astype(F32)
    ).astype(BF16)
    hidden_chip = by_core(hidden, swap_cores(hidden), 0)
    hidden_rows = half(
        hidden_chip.reshape(2, 2, 32, 384).transpose(1, 0, 2, 3).reshape(128, 384)
    )
    routed = jnp.dot(pick_routed, hidden_chip, preferred_element_type=F32).astype(BF16)
    mine = lax.all_to_all(
        routed.reshape(8, 32, 384), "tensor", split_axis=0, concat_axis=0, tiled=True
    ).reshape(256, 384)

    a, b = mine[:128], mine[128:]
    got = lax.optimization_barrier(
        [lax.ppermute(a, "dp", SHIFT_X[d]) for d in (1, 2, 3)]
        + [lax.ppermute(b, "dp", SHIFT_Y[d]) for d in (1, 2, 3)]
    )
    stack_a, stack_b = jnp.stack([a] + got[:3]), jnp.stack([b] + got[3:])
    gate_w, up_w, down_w = gate_weight[0], up_weight[0], down_weight[0]
    a1, a3, b1, b3 = [lax.ppermute(stack_a, "dp", SHIFT_Y[d]) for d in (1, 3)] + [
        lax.ppermute(stack_b, "dp", SHIFT_X[d]) for d in (1, 3)
    ]
    far_a, far_b, a1, b1 = lax.optimization_barrier((stack_a, stack_b, a1, b1))
    a2, b2 = lax.ppermute(far_a, "dp", SHIFT_Y[2]), lax.ppermute(far_b, "dp", SHIFT_X[2])
    gain = norm_gain.reshape(16, 1, 384)
    halves = [
        local_call(norm_kernel(h), [((128, 6144), BF16)], "norm", pos, *stacks, gain)[0]
        for h, stacks in ((0, (stack_a, a1, a2, a3)), (1, (stack_b, b1, b2, b3)))
    ]
    halves_other = [swap_cores(rows) for rows in halves]
    normed = jnp.concatenate(halves)

    def expert_in(rows):
        gate = jnp.dot(rows, gate_w, preferred_element_type=F32)
        up = jnp.dot(rows, up_w, preferred_element_type=F32)
        return (jax.nn.silu(gate) * up).astype(BF16)

    def expert_out_of(rows):
        return jnp.dot(rows, down_w, preferred_element_type=F32).astype(BF16)

    logits = jnp.dot(normed, router_weight, preferred_element_type=F32)
    shares = jax.nn.sigmoid(jnp.sum(logits * signs, axis=1, keepdims=True))
    inner, halves_other[0] = lax.optimization_barrier((expert_in(normed), halves_other[0]))
    other = []
    for rows in halves_other:
        inner_other = lax.optimization_barrier(expert_in(rows))
        other.append(swap_cores(expert_out_of(inner_other)))
    own = expert_out_of(inner)

    expert_out = []
    for h in (0, 1):
        near, far = (SHIFT_Y, SHIFT_X) if h == 0 else (SHIFT_X, SHIFT_Y)
        stack = (4, 128, 384)
        sums = local_call(
            combine_kernel(h),
            [(stack, BF16)] * 4,
            "combine_cores",
            pos,
            own,
            other[h],
        )
        got = [lax.ppermute(sums[d], "dp", near[d]) for d in (1, 3, 2)]
        rows = local_call(
            rows_kernel,
            [((128, 384), F32)] + [((128, 384), BF16)] * 3,
            "sum_rows",
            sums[0],
            *got,
            smem=False,
        )
        got = [lax.ppermute(rows[d], "dp", far[d]) for d in (1, 3, 2)]
        expert_out.append(rows[0] + sum(g.astype(F32) for g in got))
    expert_out = jnp.concatenate(expert_out)

    parts = (shares * expert_out).astype(BF16)
    back = lax.all_to_all(
        parts.reshape(8, 32, 384), "tensor", split_axis=0, concat_axis=0, tiled=True
    ).reshape(256, 384)
    keep = half(back)
    taken = swap_cores(jnp.where(first_core, back[:, 192:], back[:, :192]))

    def spread(pick, rows):
        return lax.dot_general(pick, rows, (((0,), (0,)), ((), ())), preferred_element_type=F32)

    return (hidden_rows.astype(F32) + spread(pick_own, keep) + spread(pick_other, taken)).astype(
        BF16
    )


def solution(mesh):
    return jax.shard_map(
        shards,
        mesh=mesh,
        in_specs=(
            P(("dp", "side"), "tensor"),
            P(("dp", "side"), "tensor"),
            P(("dp", "side"), "tensor"),
            P(("dp", "side"), None, "tensor"),
            P(("dp", "side"), None, "tensor"),
            P(("dp", "side")),
            P("tensor", ("dp", "side")),
            P("tensor", ("dp", "side")),
            P(),
            P(),
            P(),
            P("tensor", None, ("dp", "side")),
            P("tensor", None, ("dp", "side")),
            P("tensor", ("dp", "side"), None),
        ),
        out_specs=P("tensor", ("dp", "side")),
        check_vma=False,
    )
```

```python
import jax
import jax.numpy as jnp
from jax import lax
from jax.experimental import pallas as pl
from jax.experimental.pallas import tpu as pltpu
from jax.sharding import PartitionSpec as P

HEAD_DIM = 128
EXPERTS = 8
eps = 1e-05
F32 = jnp.float32
BF16 = jnp.bfloat16
VMEM_LIMIT = 16 * 1024 * 1024
ALL_VMEM = 60 * 1024 * 1024

SHIFT_X = [[(4 * x + y, 4 * ((x + d) % 4) + y) for x in range(4) for y in range(4)] for d in range(4)]
SHIFT_Y = [[(4 * x + y, 4 * x + (y + d) % 4) for x in range(4) for y in range(4)] for d in range(4)]
SWAP = [(0, 1), (1, 0)]


def swap_cores(a):
    return lax.ppermute(a, "side", SWAP)


def chip_at(pos, dx, dy):
    return ((pos[0] + dx) & 3) * 4 + ((pos[1] + dy) & 3)


def outproj_kernel(pos, g0, g1, g2, g3, w_own, w_other, out, w):
    core = pos[2]
    w[pl.ds(pl.multiple_of(core * 192, 64), 192), :] = w_own[...]
    w[pl.ds(pl.multiple_of((1 - core) * 192, 64), 192), :] = w_other[...]
    for dy, ref in enumerate((g0, g1, g2, g3)):
        sums = lax.dot_general(
            ref[...].reshape(128, 768),
            w[...],
            (((1,), (1,)), ((), ())),
            preferred_element_type=F32,
        ).astype(BF16)
        for dx in range(4):
            chip = chip_at(pos, -dx, -dy)
            row = pl.multiple_of((chip & 1) * 32, 32)
            out[chip // 2, pl.ds(row, 32), :] = sums[dx * 32 : dx * 32 + 32]


def at_half(pos, h, i, shift):
    return chip_at(pos, i, shift) if h == 0 else chip_at(pos, shift, i)


def norm_kernel(h):
    def kernel(pos, s0, s1, s2, s3, gain, out):
        refs = (s0, s1, s2, s3)

        def rows_of(n, _):
            rows = pl.ds(pl.multiple_of(n * 32, 32), 32)

            def square(j, total):
                for i in range(4):
                    v = refs[i][j, rows, :].astype(F32)
                    total = total + v * v
                return total

            squares = lax.fori_loop(0, 4, square, jnp.zeros((32, 384), F32))
            mean = jnp.sum(squares, axis=1, keepdims=True) * (1.0 / 6144.0)
            scale = lax.rsqrt(mean + eps)

            def store(j, _):
                for i in range(4):
                    chip = at_half(pos, h, -j, -i)
                    columns = pl.ds(pl.multiple_of(chip * 384, 128), 384)
                    v = refs[i][j, rows, :].astype(F32)
                    out[rows, columns] = (v * scale * gain[chip]).astype(BF16)
                return 0

            lax.fori_loop(0, 4, store, 0)
            return 0

        lax.fori_loop(0, 4, rows_of, 0)

    return kernel


def combine_kernel(h):
    def kernel(pos, own, other, *outs):
        def work(i, _):
            for k in range(4):
                columns = pl.ds(pl.multiple_of(at_half(pos, h, i, k) * 384, 128), 384)
                outs[k][i] = own[h * 128 : h * 128 + 128, columns] + other[:, columns]
            return 0

        lax.fori_loop(0, 4, work, 0)

    return kernel


def rows_kernel(mine, got1, got2, got3, *outs):
    def work(n, _):
        rows = pl.ds(pl.multiple_of(n * 32, 32), 32)
        for i in range(4):
            total = mine[i, rows, :].astype(F32)
            for got in (got1, got2, got3):
                total = total + got[i, rows, :].astype(F32)
            outs[i][rows, :] = total.astype(outs[i].dtype)
        return 0

    lax.fori_loop(0, 4, work, 0)


def local_call(kernel, outs, name, *args, smem=True):
    vmem = pl.BlockSpec(memory_space=pltpu.VMEM)
    first = [pl.BlockSpec(memory_space=pltpu.SMEM)] if smem else []
    return pl.pallas_call(
        kernel,
        in_specs=first + [vmem] * (len(args) - len(first)),
        out_specs=[vmem] * len(outs),
        out_shape=[jax.ShapeDtypeStruct(*o) for o in outs],
        compiler_params=pltpu.CompilerParams(vmem_limit_bytes=VMEM_LIMIT),
        name=name,
    )(*args)


def attend_kernel(lengths, q_in, k_in, v_in, keys, values, out, *scratch):
    q, k_new, v_new, k, v, q_heads, o_heads, sems, block_sems = scratch
    inv_root = HEAD_DIM ** (-0.5)
    small = [
        pltpu.make_async_copy(ref, to, sems.at[n])
        for n, (ref, to) in enumerate(((q_in, q), (k_in, k_new), (v_in, v_new)))
    ]

    def block_copies(b):
        rows = pl.ds(pl.multiple_of(b * 16, 16), 16)
        return (
            pltpu.make_async_copy(keys.at[rows], k.at[rows], block_sems.at[b, 0]),
            pltpu.make_async_copy(values.at[rows], v.at[rows], block_sems.at[b, 1]),
        )

    for copy in small:
        copy.start()
    for b in range(2):
        for copy in block_copies(b):
            copy.start()
    for copy in small:
        copy.wait()

    def block(b, _):
        rows = pl.ds(pl.multiple_of(b * 16, 16), 16)
        for h in range(8):
            to = pl.ds(h, 16, stride=8)
            if h < 6:
                q_heads[to, :] = q[rows, h * 128 : h * 128 + 128].astype(F32)
            else:
                q_heads[to, :] = jnp.zeros((16, 128), F32)
        queries = q_heads[...]
        own_products = queries.reshape(16, 8, 128) * k_new[rows, :].astype(F32)[:, None, :]
        own_scores = jnp.sum(own_products, axis=2, keepdims=True) * inv_root
        narrow = queries.astype(BF16)
        position = lax.broadcasted_iota(jnp.int32, (8, 192), 1)
        key_copy, value_copy = block_copies(b)
        key_copy.wait()
        scores = []
        for r in range(16):
            products = lax.dot_general(
                narrow[r * 8 : r * 8 + 8],
                k[b * 16 + r],
                (((1,), (1,)), ((), ())),
                preferred_element_type=F32,
            )
            live = position < lengths[b * 16 + r]
            scores.append(jnp.where(live, products * inv_root, -1e30))
        scores = jnp.concatenate(scores, axis=0).reshape(16, 8, 192)
        peak = jnp.maximum(jnp.max(scores, axis=2, keepdims=True), own_scores)
        weights = jnp.exp(scores - peak)
        own_weights = jnp.exp(own_scores - peak)
        scale = 1.0 / (jnp.sum(weights, axis=2, keepdims=True) + own_weights)
        weights = (weights * scale).astype(BF16).reshape(128, 192)
        own_weights = (own_weights * scale).astype(BF16).astype(F32)
        own_part = own_weights * v_new[rows, :].astype(F32)[:, None, :]
        value_copy.wait()
        for r in range(16):
            mixed = jnp.dot(
                weights[r * 8 : r * 8 + 8], v[b * 16 + r], preferred_element_type=F32
            )
            o_heads[r * 8 : r * 8 + 8, :] = mixed + own_part[r]
        for h in range(6):
            heads = o_heads[pl.ds(h, 16, stride=8), :]
            out[rows, h * 128 : h * 128 + 128] = heads.astype(BF16)
        return 0

    lax.fori_loop(0, 2, block, 0)


def attend(q_new, k_new, v_new, k_cache, v_cache, lengths):
    hbm = pl.BlockSpec(memory_space=pltpu.HBM)
    return pl.pallas_call(
        attend_kernel,
        in_specs=[pl.BlockSpec(memory_space=pltpu.SMEM)] + [hbm] * 5,
        out_specs=pl.BlockSpec(memory_space=pltpu.VMEM),
        out_shape=jax.ShapeDtypeStruct((32, 768), BF16),
        scratch_shapes=[
            pltpu.VMEM((32, 768), BF16),
            pltpu.VMEM((32, 128), BF16),
            pltpu.VMEM((32, 128), BF16),
            pltpu.VMEM((32, 192, 128), BF16),
            pltpu.VMEM((32, 192, 128), BF16),
            pltpu.VMEM((128, 128), F32),
            pltpu.VMEM((128, 128), F32),
            pltpu.SemaphoreType.DMA((3,)),
            pltpu.SemaphoreType.DMA((2, 2)),
        ],
        compiler_params=pltpu.CompilerParams(vmem_limit_bytes=ALL_VMEM),
        name="attend",
    )(lengths, q_new, k_new, v_new, k_cache, v_cache)


def ranks_of(member):
    n = member.shape[0]
    lower = (
        lax.broadcasted_iota(jnp.int32, (n, n), 0) >= lax.broadcasted_iota(jnp.int32, (n, n), 1)
    ).astype(BF16)
    counts = jnp.dot(lower, member.astype(BF16), preferred_element_type=F32).astype(jnp.int32)
    return jnp.where(member, counts - 1, -1)


def shards(
    q_new,
    k_new,
    v_new,
    k_cache,
    v_cache,
    lengths,
    attn_out_weight,
    residual,
    norm_gain,
    router_weight,
    expert_ids,
    gate_weight,
    up_weight,
    down_weight,
):
    chip = lax.axis_index("dp")
    core = lax.axis_index("side")
    plane = lax.axis_index("tensor")
    pos = jnp.stack([chip // 4, chip % 4, core]).astype(jnp.int32)
    first_core = core == 0

    def by_core(own, other, axis):
        return jnp.where(
            first_core,
            jnp.concatenate([own, other], axis=axis),
            jnp.concatenate([other, own], axis=axis),
        )

    def half(a):
        return jnp.where(first_core, a[:, :192], a[:, 192:])

    attention = attend(q_new, k_new, v_new, k_cache, v_cache, lengths)
    residual_chip = by_core(residual, swap_cores(residual), 1).reshape(2, 2, 32, 384)
    residual_half = jnp.where(first_core, residual_chip[:, 0], residual_chip[:, 1])

    labels = jnp.arange(EXPERTS, dtype=jnp.int32)
    block_ids = lax.dynamic_slice_in_dim(expert_ids, plane * 128, 128, 0)
    member = jnp.any(block_ids[:, :, None] == labels, axis=1)
    ranks = ranks_of(member).T
    ranks_by_core = ranks.reshape(8, 2, 2, 32).transpose(0, 2, 1, 3).reshape(8, 128)
    slots = jnp.arange(32, dtype=jnp.int32)

    def pick(ranks, side):
        return (ranks[:, None, :] - side * 32 == slots[:, None]).astype(BF16).reshape(256, 128)

    pick_routed = pick(ranks_by_core, core)
    pick_own, pick_other = pick(ranks, core), pick(ranks, 1 - core)
    ids_by_block = expert_ids.reshape(8, 128, 2)
    named = jnp.any(ids_by_block == plane, axis=2)
    ranks_mine = ranks_of(named.T).T
    partner_ids = jnp.sum(ids_by_block, axis=2) - plane
    hits = ranks_mine[:, None, :] - core * 32 == slots[:, None]
    partner = jnp.sum(jnp.where(hits, partner_ids[:, None, :], 0), axis=2).reshape(256, 1)
    signs = (labels == plane).astype(F32) - (labels == partner).astype(F32)

    rows_x = [lax.ppermute(attention, "dp", SHIFT_X[d]) for d in (1, 2, 3)]
    out_w = attn_out_weight.T
    out_w_other = swap_cores(out_w)
    rows_x = jnp.stack([attention] + rows_x)
    rows_xy = [rows_x] + [lax.ppermute(rows_x, "dp", SHIFT_Y[d]) for d in (1, 2, 3)]
    vmem = pl.BlockSpec(memory_space=pltpu.VMEM)
    head_sums = pl.pallas_call(
        outproj_kernel,
        in_specs=[pl.BlockSpec(memory_space=pltpu.SMEM)] + [vmem] * 6,
        out_specs=vmem,
        out_shape=jax.ShapeDtypeStruct((8, 64, 384), BF16),
        scratch_shapes=[pltpu.VMEM((384, 768), BF16)],
        compiler_params=pltpu.CompilerParams(vmem_limit_bytes=VMEM_LIMIT),
        name="out_projection",
    )(pos, *rows_xy, out_w, out_w_other)
    heads_in = lax.all_to_all(head_sums, "tensor", split_axis=0, concat_axis=0, tiled=True)
    hidden = (
        jnp.sum(heads_in.astype(F32), axis=0) + residual_half.reshape(64, 384).astype(F32)
    ).astype(BF16)
    hidden_chip = by_core(hidden, swap_cores(hidden), 0)
    hidden_rows = half(
        hidden_chip.reshape(2, 2, 32, 384).transpose(1, 0, 2, 3).reshape(128, 384)
    )
    routed = jnp.dot(pick_routed, hidden_chip, preferred_element_type=F32).astype(BF16)
    mine = lax.all_to_all(
        routed.reshape(8, 32, 384), "tensor", split_axis=0, concat_axis=0, tiled=True
    ).reshape(256, 384)

    a, b = mine[:128], mine[128:]
    got = lax.optimization_barrier(
        [lax.ppermute(a, "dp", SHIFT_X[d]) for d in (1, 2, 3)]
        + [lax.ppermute(b, "dp", SHIFT_Y[d]) for d in (1, 2, 3)]
    )
    stack_a, stack_b = jnp.stack([a] + got[:3]), jnp.stack([b] + got[3:])
    gate_w, up_w, down_w = gate_weight[0], up_weight[0], down_weight[0]
    a1, a3, b1, b3 = [lax.ppermute(stack_a, "dp", SHIFT_Y[d]) for d in (1, 3)] + [
        lax.ppermute(stack_b, "dp", SHIFT_X[d]) for d in (1, 3)
    ]
    far_a, far_b, a1, b1 = lax.optimization_barrier((stack_a, stack_b, a1, b1))
    a2, b2 = lax.ppermute(far_a, "dp", SHIFT_Y[2]), lax.ppermute(far_b, "dp", SHIFT_X[2])
    a2, b2, a3, b3 = lax.optimization_barrier((a2, b2, a3, b3))
    gain = norm_gain.reshape(16, 1, 384)
    halves = [
        local_call(norm_kernel(h), [((128, 6144), BF16)], "norm", pos, *stacks, gain)[0]
        for h, stacks in ((0, (stack_a, a1, a2, a3)), (1, (stack_b, b1, b2, b3)))
    ]
    halves_other = [swap_cores(rows) for rows in halves]
    normed = jnp.concatenate(halves)

    def expert_in(rows):
        gate = jnp.dot(rows, gate_w, preferred_element_type=F32)
        up = jnp.dot(rows, up_w, preferred_element_type=F32)
        return (jax.nn.silu(gate) * up).astype(BF16)

    def expert_out_of(rows):
        return jnp.dot(rows, down_w, preferred_element_type=F32).astype(BF16)

    logits = jnp.dot(normed, router_weight, preferred_element_type=F32)
    shares = jax.nn.sigmoid(jnp.sum(logits * signs, axis=1, keepdims=True))
    inner, halves_other[0] = lax.optimization_barrier((expert_in(normed), halves_other[0]))
    other = []
    for rows in halves_other:
        inner_other = lax.optimization_barrier(expert_in(rows))
        other.append(swap_cores(expert_out_of(inner_other)))
    own = expert_out_of(inner)

    expert_out = []
    for h in (0, 1):
        near, far = (SHIFT_Y, SHIFT_X) if h == 0 else (SHIFT_X, SHIFT_Y)
        stack = (4, 128, 384)
        sums = local_call(
            combine_kernel(h),
            [(stack, BF16)] * 4,
            "combine_cores",
            pos,
            own,
            other[h],
        )
        got = [lax.ppermute(sums[d], "dp", near[d]) for d in (1, 3, 2)]
        rows = local_call(
            rows_kernel,
            [((128, 384), F32)] + [((128, 384), BF16)] * 3,
            "sum_rows",
            sums[0],
            *got,
            smem=False,
        )
        got = [lax.ppermute(rows[d], "dp", far[d]) for d in (1, 3, 2)]
        expert_out.append(rows[0] + sum(g.astype(F32) for g in got))
    expert_out = jnp.concatenate(expert_out)

    parts = (shares * expert_out).astype(BF16)
    back = lax.all_to_all(
        parts.reshape(8, 32, 384), "tensor", split_axis=0, concat_axis=0, tiled=True
    ).reshape(256, 384)
    keep = half(back)
    taken = swap_cores(jnp.where(first_core, back[:, 192:], back[:, :192]))

    def spread(pick, rows):
        return lax.dot_general(pick, rows, (((0,), (0,)), ((), ())), preferred_element_type=F32)

    return (hidden_rows.astype(F32) + spread(pick_own, keep) + spread(pick_other, taken)).astype(
        BF16
    )


def solution(mesh):
    return jax.shard_map(
        shards,
        mesh=mesh,
        in_specs=(
            P(("dp", "side"), "tensor"),
            P(("dp", "side"), "tensor"),
            P(("dp", "side"), "tensor"),
            P(("dp", "side"), None, "tensor"),
            P(("dp", "side"), None, "tensor"),
            P(("dp", "side")),
            P("tensor", ("dp", "side")),
            P("tensor", ("dp", "side")),
            P(),
            P(),
            P(),
            P("tensor", None, ("dp", "side")),
            P("tensor", None, ("dp", "side")),
            P("tensor", ("dp", "side"), None),
        ),
        out_specs=P("tensor", ("dp", "side")),
        check_vma=False,
    )
```

```python
import jax
import jax.numpy as jnp
from jax import lax
from jax.experimental import pallas as pl
from jax.experimental.pallas import tpu as pltpu
from jax.sharding import PartitionSpec as P

HEAD_DIM = 128
EXPERTS = 8
eps = 1e-05
F32 = jnp.float32
BF16 = jnp.bfloat16
VMEM_LIMIT = 16 * 1024 * 1024
ALL_VMEM = 60 * 1024 * 1024

SHIFT_X = [[(4 * x + y, 4 * ((x + d) % 4) + y) for x in range(4) for y in range(4)] for d in range(4)]
SHIFT_Y = [[(4 * x + y, 4 * x + (y + d) % 4) for x in range(4) for y in range(4)] for d in range(4)]
SWAP = [(0, 1), (1, 0)]


def swap_cores(a):
    return lax.ppermute(a, "side", SWAP)


def chip_at(pos, dx, dy):
    return ((pos[0] + dx) & 3) * 4 + ((pos[1] + dy) & 3)


def outproj_kernel(pos, g0, g1, g2, g3, w_own, w_other, out, w):
    core = pos[2]
    w[pl.ds(pl.multiple_of(core * 192, 64), 192), :] = w_own[...]
    w[pl.ds(pl.multiple_of((1 - core) * 192, 64), 192), :] = w_other[...]
    for dy, ref in enumerate((g0, g1, g2, g3)):
        sums = lax.dot_general(
            ref[...].reshape(128, 768),
            w[...],
            (((1,), (1,)), ((), ())),
            preferred_element_type=F32,
        ).astype(BF16)
        for dx in range(4):
            chip = chip_at(pos, -dx, -dy)
            row = pl.multiple_of((chip & 1) * 32, 32)
            out[chip // 2, pl.ds(row, 32), :] = sums[dx * 32 : dx * 32 + 32]


def at_half(pos, h, i, shift):
    return chip_at(pos, i, shift) if h == 0 else chip_at(pos, shift, i)


def norm_kernel(h):
    def kernel(pos, s0, s1, s2, s3, gain, out):
        refs = (s0, s1, s2, s3)

        def rows_of(n, _):
            rows = pl.ds(pl.multiple_of(n * 32, 32), 32)

            def square(j, total):
                for i in range(4):
                    v = refs[i][j, rows, :].astype(F32)
                    total = total + v * v
                return total

            squares = lax.fori_loop(0, 4, square, jnp.zeros((32, 384), F32))
            mean = jnp.sum(squares, axis=1, keepdims=True) * (1.0 / 6144.0)
            scale = lax.rsqrt(mean + eps)

            def store(j, _):
                for i in range(4):
                    chip = at_half(pos, h, -j, -i)
                    columns = pl.ds(pl.multiple_of(chip * 384, 128), 384)
                    v = refs[i][j, rows, :].astype(F32)
                    out[rows, columns] = (v * scale * gain[chip]).astype(BF16)
                return 0

            lax.fori_loop(0, 4, store, 0)
            return 0

        lax.fori_loop(0, 4, rows_of, 0)

    return kernel


def combine_kernel(h):
    def kernel(pos, own, other, *outs):
        def work(i, _):
            for k in range(4):
                columns = pl.ds(pl.multiple_of(at_half(pos, h, i, k) * 384, 128), 384)
                outs[k][i] = own[h * 128 : h * 128 + 128, columns] + other[:, columns]
            return 0

        lax.fori_loop(0, 4, work, 0)

    return kernel


def rows_kernel(mine, got1, got2, got3, *outs):
    def work(n, _):
        rows = pl.ds(pl.multiple_of(n * 32, 32), 32)
        for i in range(4):
            total = mine[i, rows, :].astype(F32)
            for got in (got1, got2, got3):
                total = total + got[i, rows, :].astype(F32)
            outs[i][rows, :] = total.astype(outs[i].dtype)
        return 0

    lax.fori_loop(0, 4, work, 0)


def local_call(kernel, outs, name, *args, smem=True):
    vmem = pl.BlockSpec(memory_space=pltpu.VMEM)
    first = [pl.BlockSpec(memory_space=pltpu.SMEM)] if smem else []
    return pl.pallas_call(
        kernel,
        in_specs=first + [vmem] * (len(args) - len(first)),
        out_specs=[vmem] * len(outs),
        out_shape=[jax.ShapeDtypeStruct(*o) for o in outs],
        compiler_params=pltpu.CompilerParams(vmem_limit_bytes=VMEM_LIMIT),
        name=name,
    )(*args)


def attend_kernel(lengths, q_in, k_in, v_in, keys, values, out, *scratch):
    q, k_new, v_new, k, v, q_heads, o_heads, sems, block_sems = scratch
    inv_root = HEAD_DIM ** (-0.5)
    small = [
        pltpu.make_async_copy(ref, to, sems.at[n])
        for n, (ref, to) in enumerate(((q_in, q), (k_in, k_new), (v_in, v_new)))
    ]

    def block_copies(b, which):
        ref, to = ((keys, k), (values, v))[which]
        rows = [pl.ds(pl.multiple_of(b * 16, 16) + n * 4, 4) for n in range(4)]
        return [
            pltpu.make_async_copy(ref.at[rows[n]], to.at[rows[n]], block_sems.at[b, which, n])
            for n in range(4)
        ]

    for copy in small:
        copy.start()
    for b in range(2):
        for copy in block_copies(b, 0) + block_copies(b, 1):
            copy.start()
    for copy in small:
        copy.wait()

    def block(b, _):
        rows = pl.ds(pl.multiple_of(b * 16, 16), 16)
        for h in range(8):
            to = pl.ds(h, 16, stride=8)
            if h < 6:
                q_heads[to, :] = q[rows, h * 128 : h * 128 + 128].astype(F32)
            else:
                q_heads[to, :] = jnp.zeros((16, 128), F32)
        queries = q_heads[...]
        own_products = queries.reshape(16, 8, 128) * k_new[rows, :].astype(F32)[:, None, :]
        own_scores = jnp.sum(own_products, axis=2, keepdims=True) * inv_root
        narrow = queries.astype(BF16)
        position = lax.broadcasted_iota(jnp.int32, (8, 192), 1)
        for copy in block_copies(b, 0):
            copy.wait()
        scores = []
        for r in range(16):
            products = lax.dot_general(
                narrow[r * 8 : r * 8 + 8],
                k[b * 16 + r],
                (((1,), (1,)), ((), ())),
                preferred_element_type=F32,
            )
            live = position < lengths[b * 16 + r]
            scores.append(jnp.where(live, products * inv_root, -1e30))
        scores = jnp.concatenate(scores, axis=0).reshape(16, 8, 192)
        peak = jnp.maximum(jnp.max(scores, axis=2, keepdims=True), own_scores)
        weights = jnp.exp(scores - peak)
        own_weights = jnp.exp(own_scores - peak)
        scale = 1.0 / (jnp.sum(weights, axis=2, keepdims=True) + own_weights)
        weights = (weights * scale).astype(BF16).reshape(128, 192)
        own_weights = (own_weights * scale).astype(BF16).astype(F32)
        own_part = own_weights * v_new[rows, :].astype(F32)[:, None, :]
        for copy in block_copies(b, 1):
            copy.wait()
        for r in range(16):
            mixed = jnp.dot(
                weights[r * 8 : r * 8 + 8], v[b * 16 + r], preferred_element_type=F32
            )
            o_heads[r * 8 : r * 8 + 8, :] = mixed + own_part[r]
        for h in range(6):
            heads = o_heads[pl.ds(h, 16, stride=8), :]
            out[rows, h * 128 : h * 128 + 128] = heads.astype(BF16)
        return 0

    lax.fori_loop(0, 2, block, 0)


def attend(q_new, k_new, v_new, k_cache, v_cache, lengths):
    hbm = pl.BlockSpec(memory_space=pltpu.HBM)
    return pl.pallas_call(
        attend_kernel,
        in_specs=[pl.BlockSpec(memory_space=pltpu.SMEM)] + [hbm] * 5,
        out_specs=pl.BlockSpec(memory_space=pltpu.VMEM),
        out_shape=jax.ShapeDtypeStruct((32, 768), BF16),
        scratch_shapes=[
            pltpu.VMEM((32, 768), BF16),
            pltpu.VMEM((32, 128), BF16),
            pltpu.VMEM((32, 128), BF16),
            pltpu.VMEM((32, 192, 128), BF16),
            pltpu.VMEM((32, 192, 128), BF16),
            pltpu.VMEM((128, 128), F32),
            pltpu.VMEM((128, 128), F32),
            pltpu.SemaphoreType.DMA((3,)),
            pltpu.SemaphoreType.DMA((2, 2, 4)),
        ],
        compiler_params=pltpu.CompilerParams(vmem_limit_bytes=ALL_VMEM),
        name="attend",
    )(lengths, q_new, k_new, v_new, k_cache, v_cache)


def ranks_of(member):
    n = member.shape[0]
    lower = (
        lax.broadcasted_iota(jnp.int32, (n, n), 0) >= lax.broadcasted_iota(jnp.int32, (n, n), 1)
    ).astype(BF16)
    counts = jnp.dot(lower, member.astype(BF16), preferred_element_type=F32).astype(jnp.int32)
    return jnp.where(member, counts - 1, -1)


def shards(
    q_new,
    k_new,
    v_new,
    k_cache,
    v_cache,
    lengths,
    attn_out_weight,
    residual,
    norm_gain,
    router_weight,
    expert_ids,
    gate_weight,
    up_weight,
    down_weight,
):
    chip = lax.axis_index("dp")
    core = lax.axis_index("side")
    plane = lax.axis_index("tensor")
    pos = jnp.stack([chip // 4, chip % 4, core]).astype(jnp.int32)
    first_core = core == 0

    def by_core(own, other, axis):
        return jnp.where(
            first_core,
            jnp.concatenate([own, other], axis=axis),
            jnp.concatenate([other, own], axis=axis),
        )

    def half(a):
        return jnp.where(first_core, a[:, :192], a[:, 192:])

    attention = attend(q_new, k_new, v_new, k_cache, v_cache, lengths)
    residual_chip = by_core(residual, swap_cores(residual), 1).reshape(2, 2, 32, 384)
    residual_half = jnp.where(first_core, residual_chip[:, 0], residual_chip[:, 1])

    labels = jnp.arange(EXPERTS, dtype=jnp.int32)
    block_ids = lax.dynamic_slice_in_dim(expert_ids, plane * 128, 128, 0)
    member = jnp.any(block_ids[:, :, None] == labels, axis=1)
    ranks = ranks_of(member).T
    ranks_by_core = ranks.reshape(8, 2, 2, 32).transpose(0, 2, 1, 3).reshape(8, 128)
    slots = jnp.arange(32, dtype=jnp.int32)

    def pick(ranks, side):
        return (ranks[:, None, :] - side * 32 == slots[:, None]).astype(BF16).reshape(256, 128)

    pick_routed = pick(ranks_by_core, core)
    pick_own, pick_other = pick(ranks, core), pick(ranks, 1 - core)
    ids_by_block = expert_ids.reshape(8, 128, 2)
    named = jnp.any(ids_by_block == plane, axis=2)
    ranks_mine = ranks_of(named.T).T
    partner_ids = jnp.sum(ids_by_block, axis=2) - plane
    hits = ranks_mine[:, None, :] - core * 32 == slots[:, None]
    partner = jnp.sum(jnp.where(hits, partner_ids[:, None, :], 0), axis=2).reshape(256, 1)
    signs = (labels == plane).astype(F32) - (labels == partner).astype(F32)

    rows_x = [lax.ppermute(attention, "dp", SHIFT_X[d]) for d in (1, 2, 3)]
    out_w = attn_out_weight.T
    out_w_other = swap_cores(out_w)
    rows_x = jnp.stack([attention] + rows_x)
    rows_xy = [rows_x] + [lax.ppermute(rows_x, "dp", SHIFT_Y[d]) for d in (1, 2, 3)]
    vmem = pl.BlockSpec(memory_space=pltpu.VMEM)
    head_sums = pl.pallas_call(
        outproj_kernel,
        in_specs=[pl.BlockSpec(memory_space=pltpu.SMEM)] + [vmem] * 6,
        out_specs=vmem,
        out_shape=jax.ShapeDtypeStruct((8, 64, 384), BF16),
        scratch_shapes=[pltpu.VMEM((384, 768), BF16)],
        compiler_params=pltpu.CompilerParams(vmem_limit_bytes=VMEM_LIMIT),
        name="out_projection",
    )(pos, *rows_xy, out_w, out_w_other)
    heads_in = lax.all_to_all(head_sums, "tensor", split_axis=0, concat_axis=0, tiled=True)
    hidden = (
        jnp.sum(heads_in.astype(F32), axis=0) + residual_half.reshape(64, 384).astype(F32)
    ).astype(BF16)
    hidden_chip = by_core(hidden, swap_cores(hidden), 0)
    hidden_rows = half(
        hidden_chip.reshape(2, 2, 32, 384).transpose(1, 0, 2, 3).reshape(128, 384)
    )
    routed = jnp.dot(pick_routed, hidden_chip, preferred_element_type=F32).astype(BF16)
    mine = lax.all_to_all(
        routed.reshape(8, 32, 384), "tensor", split_axis=0, concat_axis=0, tiled=True
    ).reshape(256, 384)

    a, b = mine[:128], mine[128:]
    got = lax.optimization_barrier(
        [lax.ppermute(a, "dp", SHIFT_X[d]) for d in (1, 2, 3)]
        + [lax.ppermute(b, "dp", SHIFT_Y[d]) for d in (1, 2, 3)]
    )
    stack_a, stack_b = jnp.stack([a] + got[:3]), jnp.stack([b] + got[3:])
    gate_w, up_w, down_w = gate_weight[0], up_weight[0], down_weight[0]
    a1, a3, b1, b3 = [lax.ppermute(stack_a, "dp", SHIFT_Y[d]) for d in (1, 3)] + [
        lax.ppermute(stack_b, "dp", SHIFT_X[d]) for d in (1, 3)
    ]
    far_a, far_b, a1, b1 = lax.optimization_barrier((stack_a, stack_b, a1, b1))
    a2, b2 = lax.ppermute(far_a, "dp", SHIFT_Y[2]), lax.ppermute(far_b, "dp", SHIFT_X[2])
    a2, b2, a3, b3 = lax.optimization_barrier((a2, b2, a3, b3))
    gain = norm_gain.reshape(16, 1, 384)
    halves = [
        local_call(norm_kernel(h), [((128, 6144), BF16)], "norm", pos, *stacks, gain)[0]
        for h, stacks in ((0, (stack_a, a1, a2, a3)), (1, (stack_b, b1, b2, b3)))
    ]
    halves_other = [swap_cores(rows) for rows in halves]
    normed = jnp.concatenate(halves)

    def expert_in(rows):
        gate = jnp.dot(rows, gate_w, preferred_element_type=F32)
        up = jnp.dot(rows, up_w, preferred_element_type=F32)
        return (jax.nn.silu(gate) * up).astype(BF16)

    def expert_out_of(rows):
        return jnp.dot(rows, down_w, preferred_element_type=F32).astype(BF16)

    logits = jnp.dot(normed, router_weight, preferred_element_type=F32)
    shares = jax.nn.sigmoid(jnp.sum(logits * signs, axis=1, keepdims=True))
    inner, halves_other[0] = lax.optimization_barrier((expert_in(normed), halves_other[0]))
    other = []
    for rows in halves_other:
        inner_other = lax.optimization_barrier(expert_in(rows))
        other.append(swap_cores(expert_out_of(inner_other)))
    own = expert_out_of(inner)

    expert_out = []
    for h in (0, 1):
        near, far = (SHIFT_Y, SHIFT_X) if h == 0 else (SHIFT_X, SHIFT_Y)
        stack = (4, 128, 384)
        sums = local_call(
            combine_kernel(h),
            [(stack, BF16)] * 4,
            "combine_cores",
            pos,
            own,
            other[h],
        )
        got = [lax.ppermute(sums[d], "dp", near[d]) for d in (1, 3, 2)]
        rows = local_call(
            rows_kernel,
            [((128, 384), F32)] + [((128, 384), BF16)] * 3,
            "sum_rows",
            sums[0],
            *got,
            smem=False,
        )
        got = [lax.ppermute(rows[d], "dp", far[d]) for d in (1, 3, 2)]
        expert_out.append(rows[0] + sum(g.astype(F32) for g in got))
    expert_out = jnp.concatenate(expert_out)

    parts = (shares * expert_out).astype(BF16)
    back = lax.all_to_all(
        parts.reshape(8, 32, 384), "tensor", split_axis=0, concat_axis=0, tiled=True
    ).reshape(256, 384)
    keep = half(back)
    taken = swap_cores(jnp.where(first_core, back[:, 192:], back[:, :192]))

    def spread(pick, rows):
        return lax.dot_general(pick, rows, (((0,), (0,)), ((), ())), preferred_element_type=F32)

    return (hidden_rows.astype(F32) + spread(pick_own, keep) + spread(pick_other, taken)).astype(
        BF16
    )


def solution(mesh):
    return jax.shard_map(
        shards,
        mesh=mesh,
        in_specs=(
            P(("dp", "side"), "tensor"),
            P(("dp", "side"), "tensor"),
            P(("dp", "side"), "tensor"),
            P(("dp", "side"), None, "tensor"),
            P(("dp", "side"), None, "tensor"),
            P(("dp", "side")),
            P("tensor", ("dp", "side")),
            P("tensor", ("dp", "side")),
            P(),
            P(),
            P(),
            P("tensor", None, ("dp", "side")),
            P("tensor", None, ("dp", "side")),
            P("tensor", ("dp", "side"), None),
        ),
        out_specs=P("tensor", ("dp", "side")),
        check_vma=False,
    )
```
